256 devices in a mesh: row: 8 (over x, y_lo), col: 32 (over z, y_hi, core).
Axes of the slice: x: 4, y: 4 (y_hi: 2, y_lo: 2; y = y_hi * 2 + y_lo), z: 8, core: 2. Of those that a mesh axis runs over, the one named last changes fastest.
Arguments:
- ancestor_inverse: float32 [16384, 16384], P('row', 'col'), may hold values from -6 to 6
- panel: float32 [6, 64, 256, 256], P(None, 'row', 'col'), may hold values from -0.0625 to 0.0625
- diag_inverse: float32 [6, 256, 256], replicated, as said below
- structure: int32 [6, 32], replicated, may hold values from 0 to 63, as said below
- block_slot: int32 [64], replicated, may hold values from 0 to 63, as said below
Outputs:
- off_block: float32 [6, 64, 256, 256], P(None, 'row', 'col')
- diag_block: float32 [6, 256, 256], replicated
The draws below stay inside these ranges and needn't reach their ends.
Inputs may be any that keep to these rules, and one draw needn't show every extreme that they name: `structure`: the 32 entries of a supernode are distinct global row blocks. Mapped through block_slot, at most 6 of them fall into any aligned run of 8 storage slots, and for every supernode some run holds exactly 6. `block_slot`: A permutation of the 64 row blocks. `diag_inverse`: lower triangular with a positive diagonal.
All inputs are finite; a program needn't handle non-finite values.
Results may differ from the reference program's by a relative error of at most 0.0001.
Values sent between devices are 32-bit elements; how exact they have to be, the bound alone decides.
A program may use at most 128 MiB of HBM per device.

```python
import jax
import jax.numpy as jnp
from jax import lax

W = 256
SLOTS_ROW = 8
CAP = 6
S = 6
NB = 64
R = 32


def draw_pattern(key):
    row_groups = NB // SLOTS_ROW
    half_row = SLOTS_ROW // 2
    reach = CAP - half_row
    pair_count = row_groups // 2
    base_key = jax.random.fold_in(key, 101)
    key_shift, key_forced, key_sign, key_score, key_perm = jax.random.split(base_key, 5)
    shift = jax.random.randint(key_shift, (S, pair_count), -reach, reach + 1)
    forced = jax.random.randint(key_forced, (S,), 0, pair_count)
    signs = jax.random.randint(key_sign, (S,), 0, 2) * 2 - 1
    pair_index = jnp.arange(pair_count, dtype=jnp.int32)[None, :]
    shift = jnp.where(pair_index == forced[:, None], reach * signs[:, None], shift)
    counts = jnp.stack([half_row + shift, half_row - shift], axis=-1).reshape(S, row_groups)
    scores = jax.random.randint(key_score, (S, row_groups, SLOTS_ROW), 0, 1 << 20) * SLOTS_ROW + jnp.arange(SLOTS_ROW, dtype=jnp.int32)
    ranks = jnp.sum((scores[:, :, None, :] < scores[:, :, :, None]).astype(jnp.int32), axis=-1)
    picked = (ranks < counts[:, :, None]).astype(jnp.int32).reshape(S, NB)
    position = jnp.cumsum(picked, axis=1) - 1
    onehot = ((position[:, None, :] == jnp.arange(R, dtype=jnp.int32)[None, :, None]) & (picked[:, None, :] == 1)).astype(jnp.int32)
    slot_list = jnp.sum(onehot * jnp.arange(NB, dtype=jnp.int32)[None, None, :], axis=2)
    permuted = jax.random.permutation(key_perm, NB).astype(jnp.int32)
    inverse_perm = jnp.argsort(permuted).astype(jnp.int32)
    structure_ids = jnp.take(inverse_perm, slot_list, axis=0)
    return (structure_ids.astype(jnp.int32), permuted)


def draw_structure(key, part):
    structure_ids, permuted = draw_pattern(key)
    return structure_ids


def draw_block_slot(key, part):
    structure_ids, permuted = draw_pattern(key)
    return permuted


def draw_diag_inverse(key, part):
    key_lower, key_diag = jax.random.split(jax.random.fold_in(key, 7))
    lower = jax.random.normal(key_lower, (S, W, W), jnp.float32) * 0.8 / jnp.sqrt(jnp.float32(W))
    diagonal = jax.random.uniform(key_diag, (S, W, W), jnp.float32, 1.0, 2.0)
    row_ids = jnp.arange(W, dtype=jnp.int32)[:, None]
    col_ids = jnp.arange(W, dtype=jnp.int32)[None, :]
    result = jnp.where(row_ids > col_ids, lower, jnp.where(row_ids == col_ids, diagonal, 0.0))
    return result.astype(jnp.float32)


def steps_of(key, shape, shards, smallest, high):
    def one(dim, shards_of):
        draws = jax.random.uniform(jax.random.fold_in(jax.random.fold_in(key, 6), dim), (shards_of,), jnp.float32, smallest / len(shards), high / len(shards))
        return jnp.repeat(jnp.exp(draws), shape[dim] // shards_of).reshape((-1,) + (1,) * (len(shape) - dim - 1))

    gain = one(*shards[0])
    for cut in shards[1:]:
        gain = gain * one(*cut)
    return gain


def scatter_about(own_key, shape, width, most, cuts=(), held_as=jnp.bfloat16):
    values = width * jax.random.normal(own_key, shape, jnp.float32)
    if cuts:
        values = values * steps_of(own_key, shape, cuts, -0.22, 0.18)
    return jnp.clip(values, -most, most).astype(held_as)


def setup_inputs(seed: int = 0) -> dict:
    splits = jax.random.split(jax.random.key(seed), 6)
    return {
        "ancestor_inverse": scatter_about(splits[0], (NB * W, NB * W), 1.0, 6.0, ((0, 8), (1, 32)), jnp.float32),
        "panel": scatter_about(splits[1], (S, NB, W, W), (R * W) ** -0.5, 0.0625, ((1, 8), (2, 32)), jnp.float32),
        "diag_inverse": draw_diag_inverse(jax.random.fold_in(splits[5], 71), 0),
        "structure": draw_structure(jax.random.fold_in(splits[5], 71), 0),
        "block_slot": draw_block_slot(jax.random.fold_in(splits[5], 71), 0),
    }


def reference(ancestor_inverse, panel, diag_inverse, structure, block_slot):
    highest = lax.Precision.HIGHEST
    slot_ids = jnp.take(block_slot, structure, axis=0).astype(jnp.int32)
    rows_three = ancestor_inverse.reshape(NB, W, NB * W)
    off_list = []
    diag_list = []
    for node in range(S):
        chosen = slot_ids[node]
        normalized = jnp.einsum("qik,kw->qiw", jnp.take(panel[node], chosen, axis=0), diag_inverse[node], precision=highest)
        gathered = jnp.take(rows_three, chosen, axis=0).reshape(R, W, NB, W)
        gathered = jnp.take(gathered, chosen, axis=2).reshape(R * W, R * W)
        flat_panel = normalized.reshape(R * W, W)
        product = jnp.dot(gathered, flat_panel, precision=highest, preferred_element_type=jnp.float32)
        empty = jnp.zeros((NB, W, W), jnp.float32)
        off_list.append(empty.at[chosen].set(-product.reshape(R, W, W)))
        leading = jnp.dot(diag_inverse[node].T, diag_inverse[node], precision=highest, preferred_element_type=jnp.float32)
        correction = jnp.dot(flat_panel.T, product, precision=highest, preferred_element_type=jnp.float32)
        diag_list.append(leading + correction)
    return jnp.stack(off_list), jnp.stack(diag_list)
```

```python
import functools

import jax
import jax.numpy as jnp
from jax import lax
from jax.experimental import pallas as pl
from jax.experimental.pallas import tpu as pltpu
from jax.sharding import PartitionSpec as P

F32 = jnp.float32
BF16 = jnp.bfloat16
MESH = pl.DeviceIdType.MESH
HIGHEST = lax.Precision.HIGHEST

NR = 8
NZ = 8
CAP = 6
LAG = 4


def halves(value):
    high = value.astype(BF16)
    return high, (value - high.astype(F32)).astype(BF16)


def wait_for(ref, sem):
    pltpu.make_async_copy(ref, ref, sem).wait()


def kernel(
    group,
    ids, pos, mask, a_ref, panel, dinv, off, diag,
    af, ahi, alo, nsrc, nflat, abuf, nbuf, nhi, nlo, ybuf, rbuf, pbuf, yfin,
    dbuf, drow, ebuf, ez, fq, gr, lead,
    a_sem, s1_s, s1_r, s1_l, s2_s, s2_r, s2_l,
    c1_s, c1_r, c2_s, c2_r, c3_s, c3_r, sh_s, sh_r,
    ring_s, ring_r, p_s, p_r, d_s, d_r,
):
    nodes, slots, sub, width = panel.shape
    lane = width // 2
    groups = nodes // group
    r = lax.axis_index("row")
    c = lax.axis_index("col")
    z = c // 4
    yh = lax.rem(c // 2, 2)
    core = lax.rem(c, 2)
    q = lax.rem(c, 4)
    zy = c // 2
    x = r // 2
    yl = lax.rem(r, 2)

    def dev(row, zz, qq):
        return {"row": row, "col": zz * 4 + qq}

    def send(src, dst, ssem, rsem, where):
        pltpu.make_async_remote_copy(
            src_ref=src, dst_ref=dst, send_sem=ssem, recv_sem=rsem,
            device_id=where, device_id_type=MESH,
        ).start()

    mate = dev(r, z, yh * 2 + 1 - core)
    across = dev(r, z, (1 - yh) * 2 + core)

    def row_peer(i):
        return lax.rem(r + i, NR)

    def zy_peer(i):
        return lax.rem(zy + i, 2 * NZ)

    def z_peer(i):
        return lax.rem(z + i, NZ)

    own_a = pltpu.make_async_copy(a_ref.at[:, :, core], af.at[core], a_sem.at[0])
    own_a.start()

    barrier = pltpu.get_barrier_semaphore()

    def greet(where):
        pl.semaphore_signal(barrier, inc=1, device_id=where, device_id_type=MESH)

    @pl.loop(1, NR)
    def _(i):
        greet({"row": row_peer(i), "col": c})

    @pl.loop(1, 2 * NZ)
    def _(i):
        greet({"row": r, "col": zy_peer(i) * 2 + core})

    greet(mate)
    greet(dev(r, z, 3 - q))

    @pl.loop(0, nodes)
    def _(s):
        value = jnp.dot(
            panel[s].reshape(slots * sub, width), dinv[s],
            precision=HIGHEST, preferred_element_type=F32,
        )
        for k in range(slots):
            part = value[k * sub:(k + 1) * sub] * mask[s, k].astype(F32)
            nflat[s, k * sub:(k + 1) * sub, :] = part
            for h in range(2):
                nsrc[s, k // 4, (k % 4) * 2 + h] = part[:, h * lane:(h + 1) * lane]

    pl.semaphore_wait(barrier, NR - 1 + 2 * NZ - 1 + 2)

    for g in range(groups):
        span = pl.ds(g * group, group)
        pltpu.make_async_copy(nsrc.at[span, :, r], abuf.at[g, r], s1_l.at[g]).start()

        @pl.loop(1, NR)
        def _(i):
            p = row_peer(i)
            send(nsrc.at[span, :, p], abuf.at[g, r], s1_s.at[g], s1_r.at[g], {"row": p, "col": c})

    send(a_ref.at[:, :, 1 - core], af.at[core], a_sem.at[1], a_sem.at[2], mate)

    for g in range(groups):
        span = pl.ds(g * group, group)
        wait_for(abuf.at[g, r], s1_l.at[g])
        wait_for(abuf.at[g, pl.ds(0, NR - 1)], s1_r.at[g])
        pltpu.make_async_copy(abuf.at[g, z, :, yh], nbuf.at[span, r, zy, core], s2_l.at[g]).start()

        @pl.loop(1, 2 * NZ)
        def _(i):
            t = zy_peer(i)
            send(
                abuf.at[g, t // 2, :, lax.rem(t, 2)], nbuf.at[span, r, zy, core],
                s2_s.at[g], s2_r.at[g], {"row": r, "col": t * 2 + core},
            )

    @pl.loop(0, nodes)
    def _(s):
        lead[s] = lax.dot_general(
            dinv[s], dinv[s], (((0,), (0,)), ((), ())),
            precision=HIGHEST, preferred_element_type=F32,
        )

    own_a.wait()
    wait_for(af.at[1 - core], a_sem.at[2])

    @pl.loop(0, slots)
    def _(k):
        for h in range(2):
            rows, cols = ahi.shape[1], ahi.shape[2] // 2
            high, low = halves(af[h, k].reshape(rows, cols))
            ahi[k, :, h * cols:(h + 1) * cols] = high
            alo[k, :, h * cols:(h + 1) * cols] = low

    right = {"row": lax.rem(x + 1, 4) * 2 + yl, "col": c}
    left = {"row": lax.rem(x + 3, 4) * 2 + yl, "col": c}
    twin = {"row": x * 2 + 1 - yl, "col": c}
    xl, xr, xo = lax.rem(x + 3, 4), lax.rem(x + 1, 4), lax.rem(x + 2, 4)
    way = 1 - 2 * core
    onward = dev(lax.rem(r, NR), lax.rem(z + way + NZ, NZ), q)

    def block(s, p):
        return nbuf.at[s, p, :, core]

    def relay_one(s):
        @pl.when(lax.rem(s, group) == 0)
        def _():
            g = s // group
            wait_for(nbuf.at[pl.ds(0, group), r, zy, core], s2_l.at[g])
            wait_for(nbuf.at[pl.ds(0, group), r, pl.ds(0, 2 * NZ - 1), core], s2_r.at[g])
        send(block(s, r), block(s, r), c1_s.at[s], c1_r.at[s], twin)

    def relay_two(s):
        wait_for(block(s, r), c1_r.at[s])
        pair = nbuf.at[s, pl.ds(2 * x, 2), :, core]
        send(pair, pair, c2_s.at[s, 0], c2_r.at[s, 0], right)
        send(pair, pair, c2_s.at[s, 1], c2_r.at[s, 1], left)

    def relay_three(s):
        wait_for(nbuf.at[s, pl.ds(0, 2), :, core], c2_r.at[s, 0])
        send(block(s, 2 * xl), block(s, 2 * xl), c3_s.at[s, 0], c3_r.at[s, 0], right)
        wait_for(nbuf.at[s, pl.ds(0, 2), :, core], c2_r.at[s, 1])
        send(block(s, 2 * xr + 1), block(s, 2 * xr + 1), c3_s.at[s, 1], c3_r.at[s, 1], left)

    def share(s):
        wait_for(block(s, 2 * xo), c3_r.at[s, 0])
        wait_for(block(s, 2 * xo + 1), c3_r.at[s, 1])
        mine = nbuf.at[s, :, :, core]
        send(mine, mine, sh_s.at[s], sh_r.at[s], mate)

    def multiply(s):
        wait_for(nbuf.at[s, :, :, 1 - core], sh_r.at[s])
        for j in range(4):
            for h in range(2):
                high, low = halves(nbuf[s, 2 * j + h].reshape(width, lane))
                nhi[j * width:(j + 1) * width, h * lane:(h + 1) * lane] = high
                nlo[j * width:(j + 1) * width, h * lane:(h + 1) * lane] = low

        @pl.loop(0, CAP // 2)
        def _(m):
            one, two = ids[s, 2 * m], ids[s, 2 * m + 1]
            high = jnp.concatenate([ahi[one], ahi[two]], axis=0)
            low = jnp.concatenate([alo[one], alo[two]], axis=0)
            total = jnp.dot(high, nhi[...], preferred_element_type=F32)
            total += jnp.dot(high, nlo[...], preferred_element_type=F32)
            total += jnp.dot(low, nhi[...], preferred_element_type=F32)
            rows = ahi.shape[1]
            ybuf[s, :, 2 * m] = total[:rows].reshape(NZ, 2, sub, width)
            ybuf[s, :, 2 * m + 1] = total[rows:].reshape(NZ, 2, sub, width)
        b = lax.rem(z - way + NZ, NZ)
        send(ybuf.at[s, b], rbuf.at[s, 0], ring_s.at[s, 0], ring_r.at[s, 0], onward)

    def ring(s, t):
        wait_for(rbuf.at[s, t], ring_r.at[s, t])
        b = lax.rem(z - way * (t + 2) + 2 * NZ, NZ)
        ybuf[s, b] = ybuf[s, b] + rbuf[s, t]

        @pl.when(t < NZ - 2)
        def _():
            send(ybuf.at[s, b], rbuf.at[s, t + 1], ring_s.at[s, t + 1], ring_r.at[s, t + 1], onward)

        @pl.when(t == NZ - 2)
        def _():
            send(ybuf.at[s, z, :, 1 - yh], pbuf.at[s], p_s.at[s], p_r.at[s], across)

    def finish(s):
        wait_for(pbuf.at[s], p_r.at[s])
        yfin[s] = ybuf[s, z, :, yh] + pbuf[s]
        for k in range(slots):
            off[s, k] = yfin[s, pos[s, k]] * (-mask[s, k].astype(F32))
        part = -lax.dot_general(
            nflat[s], off[s].reshape(slots * sub, width), (((0,), (0,)), ((), ())),
            precision=HIGHEST, preferred_element_type=F32,
        )
        for h in range(2):
            dbuf[s, :, h * 4:(h + 1) * 4] = part[:, h * lane:(h + 1) * lane].reshape(NR, 4, sub, lane)
        drow[s, r] = dbuf[s, r]

        @pl.loop(1, NR)
        def _(i):
            p = row_peer(i)
            send(dbuf.at[s, p], drow.at[s, r], d_s.at[s, 0], d_r.at[s, 0], {"row": p, "col": c})

    def diag_z(s):
        wait_for(drow.at[s, pl.ds(0, NR - 1)], d_r.at[s, 0])
        ebuf[s] = jnp.sum(drow[s], axis=0)
        ez[s, z] = ebuf[s, z]

        @pl.loop(1, NZ)
        def _(i):
            t = z_peer(i)
            send(ebuf.at[s, t], ez.at[s, z], d_s.at[s, 1], d_r.at[s, 1], dev(r, t, q))

    def diag_q(s):
        wait_for(ez.at[s, pl.ds(0, NZ - 1)], d_r.at[s, 1])
        fq[s, q] = jnp.sum(ez[s], axis=0)
        for i in range(1, 4):
            send(fq.at[s, q], fq.at[s, q], d_s.at[s, 2], d_r.at[s, 2], dev(r, z, lax.rem(q + i, 4)))

    def spread_z(s):
        wait_for(fq.at[s, pl.ds(0, 3)], d_r.at[s, 2])
        gr[s, r, z] = (fq[s, 0] + fq[s, 1]) + (fq[s, 2] + fq[s, 3])

        @pl.loop(1, NZ)
        def _(i):
            send(gr.at[s, r, z], gr.at[s, r, z], d_s.at[s, 3], d_r.at[s, 3], dev(r, z_peer(i), q))

    def spread_row(s):
        wait_for(gr.at[s, r, pl.ds(0, NZ - 1)], d_r.at[s, 3])

        @pl.loop(1, NR)
        def _(i):
            send(gr.at[s, r], gr.at[s, r], d_s.at[s, 4], d_r.at[s, 4], {"row": row_peer(i), "col": c})

    def gather_diag(s):
        wait_for(gr.at[s, pl.ds(0, NR - 1)], d_r.at[s, 4])
        for h in range(2):
            here = slice(h * lane, (h + 1) * lane)
            diag[s, :, here] = lead[s, :, here] + gr[s, :, h * 4:(h + 1) * 4].reshape(width, lane)

    last = LAG + NZ
    after = (gather_diag, spread_row, spread_z, diag_q, diag_z, finish)
    before = (multiply, share, relay_three, relay_two, relay_one)

    @pl.loop(0, nodes + last + len(after) - 1)
    def _(n):
        def at(lag, work):
            s = n - lag

            @pl.when((s >= 0) & (s < nodes))
            def _():
                work(s)

        for i, work in enumerate(after):
            at(last + len(after) - 1 - i, work)

        @pl.loop(0, NZ - 1)
        def _(i):
            t = NZ - 2 - i
            s = n - (LAG + 1) - t

            @pl.when((s >= 0) & (s < nodes))
            def _():
                ring(s, t)

        for i, work in enumerate(before):
            at(LAG - i, work)

    wait_for(af.at[core], a_sem.at[1])
    for g in range(groups):
        wait_for(abuf.at[g, pl.ds(0, NR - 1)], s1_s.at[g])
        wait_for(nbuf.at[pl.ds(0, group), r, pl.ds(0, 2 * NZ - 1), core], s2_s.at[g])

    @pl.loop(0, nodes)
    def _(s):
        wait_for(block(s, r), c1_s.at[s])
        for w in range(2):
            wait_for(nbuf.at[s, pl.ds(0, 2), :, core], c2_s.at[s, w])
            wait_for(block(s, r), c3_s.at[s, w])
        wait_for(nbuf.at[s, :, :, core], sh_s.at[s])

        @pl.loop(0, NZ - 1)
        def _(t):
            wait_for(rbuf.at[s, t], ring_s.at[s, t])

        wait_for(pbuf.at[s], p_s.at[s])
        wait_for(drow.at[s, pl.ds(0, NR - 1)], d_s.at[s, 0])
        wait_for(ez.at[s, pl.ds(0, NZ - 1)], d_s.at[s, 1])
        wait_for(fq.at[s, pl.ds(0, 3)], d_s.at[s, 2])
        wait_for(gr.at[s, r, pl.ds(0, NZ - 1)], d_s.at[s, 3])
        wait_for(gr.at[s, pl.ds(0, NR - 1)], d_s.at[s, 4])


def body(ancestor_inverse, panel, diag_inverse, structure, block_slot):
    nodes, slots, sub, width = panel.shape
    total = slots * NR
    group = 2 if nodes % 2 == 0 else 1
    groups = nodes // group
    lane = width // 2
    r = lax.axis_index("row")
    slot_range = jnp.arange(total, dtype=jnp.int32)
    lookup = (structure[:, :, None] == slot_range[None, None, :]).astype(jnp.int32)
    slot_ids = jnp.sum(lookup * block_slot[None, None, :], axis=2)
    local = jnp.arange(slots, dtype=jnp.int32)
    near = slot_ids[:, :, None] == (local + r * slots)[None, None, :]
    mask = jnp.sum(near.astype(jnp.int32), axis=1)
    pos = jnp.sum(mask[:, None, :] * (local[None, :] < local[:, None]).astype(jnp.int32)[None], axis=2) * mask
    place = jnp.arange(CAP, dtype=jnp.int32)
    ids = jnp.sum((pos[:, None, :] == place[None, :, None]) * mask[:, None, :] * local[None, None, :], axis=2)

    blocks = ancestor_inverse.reshape(slots, 2 * NZ, 2, sub, 2 * width)
    rows, depth = slots * 0 + width // 2, 4 * width
    vmem = pl.BlockSpec(memory_space=pltpu.VMEM)
    smem = pl.BlockSpec(memory_space=pltpu.SMEM)
    dma = pltpu.SemaphoreType.DMA
    return pl.pallas_call(
        functools.partial(kernel, group),
        out_shape=(
            jax.ShapeDtypeStruct((nodes, slots, sub, width), F32),
            jax.ShapeDtypeStruct((nodes, width, width), F32),
        ),
        in_specs=[smem, smem, smem, pl.BlockSpec(memory_space=pl.ANY), vmem, vmem],
        out_specs=(vmem, vmem),
        scratch_shapes=[
            pltpu.VMEM((2, slots, 2 * NZ, sub, 2 * width), F32),
            pltpu.VMEM((slots, rows, depth), BF16),
            pltpu.VMEM((slots, rows, depth), BF16),
            pltpu.VMEM((nodes, 2, NR, sub, lane), F32),
            pltpu.VMEM((nodes, slots * sub, width), F32),
            pltpu.VMEM((groups, NR, group, 2, sub, lane), F32),
            pltpu.VMEM((nodes, NR, 2 * NZ, 2, sub, lane), F32),
            pltpu.VMEM((depth, width), BF16),
            pltpu.VMEM((depth, width), BF16),
            pltpu.VMEM((nodes, NZ, CAP, 2, sub, width), F32),
            pltpu.VMEM((nodes, NZ - 1, CAP, 2, sub, width), F32),
            pltpu.VMEM((nodes, CAP, sub, width), F32),
            pltpu.VMEM((nodes, CAP, sub, width), F32),
            pltpu.VMEM((nodes, NR, NZ, sub, lane), F32),
            pltpu.VMEM((nodes, NR, NZ, sub, lane), F32),
            pltpu.VMEM((nodes, NZ, sub, lane), F32),
            pltpu.VMEM((nodes, NZ, sub, lane), F32),
            pltpu.VMEM((nodes, 4, sub, lane), F32),
            pltpu.VMEM((nodes, NR, NZ, sub, lane), F32),
            pltpu.VMEM((nodes, width, width), F32),
            dma((3,)),
            dma((groups,)), dma((groups,)), dma((groups,)),
            dma((groups,)), dma((groups,)), dma((groups,)),
            dma((nodes,)), dma((nodes,)),
            dma((nodes, 2)), dma((nodes, 2)),
            dma((nodes, 2)), dma((nodes, 2)),
            dma((nodes,)), dma((nodes,)),
            dma((nodes, NZ - 1)), dma((nodes, NZ - 1)),
            dma((nodes,)), dma((nodes,)),
            dma((nodes, 5)), dma((nodes, 5)),
        ],
        compiler_params=pltpu.CompilerParams(
            collective_id=0, has_side_effects=True, vmem_limit_bytes=62 * 1024 * 1024
        ),
        name="invert_level",
    )(ids, pos, mask, blocks, panel, diag_inverse)


def solution(mesh):
    in_specs = (P("row", "col"), P(None, "row", "col", None), P(), P(), P())
    out_specs = (P(None, "row", "col", None), P())
    return jax.shard_map(body, mesh=mesh, in_specs=in_specs, out_specs=out_specs, check_vma=False)
```

```python
import functools

import jax
import jax.numpy as jnp
from jax import lax
from jax.experimental import pallas as pl
from jax.experimental.pallas import tpu as pltpu
from jax.sharding import PartitionSpec as P

F32 = jnp.float32
BF16 = jnp.bfloat16
MESH = pl.DeviceIdType.MESH
HIGHEST = lax.Precision.HIGHEST

NR = 8
NZ = 8
CAP = 6
LAG = 3


def halves(value):
    high = value.astype(BF16)
    return high, (value - high.astype(F32)).astype(BF16)


def wait_for(ref, sem):
    pltpu.make_async_copy(ref, ref, sem).wait()


def kernel(
    group,
    structure, place, a_ref, panel_ref, dinv_ref, off, diag,
    ids, pos, mask, panel, dinv,
    af, ahi, alo, nsrc, nboth, abuf, nbuf, nhi, nlo, ybuf, rbuf, pbuf, yfin, fexp,
    dbuf, drow, ebuf, ez, gr, lead,
    in_sem, a_sem, s1_s, s1_r, s1_l, s2_s, s2_r, s2_l,
    c1_s, c1_r, c2_s, c2_r, c3_s, c3_r, sh_s, sh_r, n_s, n_r,
    ring_s, ring_r, p_s, p_r, d_s, d_r,
):
    nodes, slots, sub, width = panel.shape
    lane = width // 2
    flat = slots * sub
    groups = nodes // group
    r = lax.axis_index("row")
    c = lax.axis_index("col")
    z = c // 4
    yh = lax.rem(c // 2, 2)
    core = lax.rem(c, 2)
    zy = c // 2
    rc = r * 2 + core
    x = r // 2
    yl = lax.rem(r, 2)

    def send(src, dst, ssem, rsem, where):
        pltpu.make_async_remote_copy(
            src_ref=src, dst_ref=dst, send_sem=ssem, recv_sem=rsem,
            device_id=where, device_id_type=MESH,
        ).start()

    def at_rc(t):
        return {"row": t // 2, "col": zy * 2 + lax.rem(t, 2)}

    def at_zy(t):
        return {"row": r, "col": t * 2 + core}

    def rc_peer(i):
        return lax.rem(rc + i, 2 * NR)

    def zy_peer(i):
        return lax.rem(zy + i, 2 * NZ)

    mate = {"row": r, "col": zy * 2 + 1 - core}
    across = at_zy(z * 2 + 1 - yh)

    load_panel = pltpu.make_async_copy(panel_ref, panel, in_sem.at[0])
    load_dinv = pltpu.make_async_copy(dinv_ref, dinv, in_sem.at[1])
    own_a = pltpu.make_async_copy(a_ref.at[:, :, core], af.at[core], a_sem.at[0])
    load_panel.start()
    load_dinv.start()
    own_a.start()

    barrier = pltpu.get_barrier_semaphore()

    @pl.loop(1, 2 * NR)
    def _(i):
        pl.semaphore_signal(barrier, inc=1, device_id=at_rc(rc_peer(i)), device_id_type=MESH)
        pl.semaphore_signal(barrier, inc=1, device_id=at_zy(zy_peer(i)), device_id_type=MESH)

    @pl.loop(0, nodes)
    def _(s):
        def count(k, seen):
            slot = place[structure[s, k]] - r * slots
            return tuple(n + (slot == i).astype(jnp.int32) for i, n in enumerate(seen))

        seen = lax.fori_loop(0, structure.shape[1], count, (jnp.int32(0),) * slots)
        before = jnp.int32(0)
        spots = []
        for i in range(slots):
            mask[s, i] = seen[i]
            pos[s, i] = before * seen[i]
            spots.append(before)
            before = before + seen[i]
        for k in range(CAP):
            found = jnp.int32(0)
            for i in range(slots):
                found = found + i * seen[i] * (spots[i] == k).astype(jnp.int32)
            ids[s, k] = found

    load_panel.wait()
    load_dinv.wait()

    @pl.loop(0, nodes)
    def _(s):
        value = jnp.dot(
            panel[s].reshape(flat, width), dinv[s],
            precision=HIGHEST, preferred_element_type=F32,
        )
        for k in range(slots):
            part = value[k * sub:(k + 1) * sub] * mask[s, k].astype(F32)
            nboth[s, 0, k * sub:(k + 1) * sub, :] = part
            for h in range(2):
                nsrc[s, k // 4, (k % 4) * 2 + h] = part[:, h * lane:(h + 1) * lane]

    pl.semaphore_wait(barrier, 2 * (2 * NR - 1))

    for g in range(groups):
        span = pl.ds(g * group, group)
        pltpu.make_async_copy(nsrc.at[span, :, r], abuf.at[g, r], s1_l.at[g]).start()

        @pl.loop(1, NR)
        def _(i):
            p = lax.rem(r + i, NR)
            send(nsrc.at[span, :, p], abuf.at[g, r], s1_s.at[g], s1_r.at[g], {"row": p, "col": c})

    send(a_ref.at[:, :, 1 - core], af.at[core], a_sem.at[1], a_sem.at[2], mate)

    for g in range(groups):
        span = pl.ds(g * group, group)
        wait_for(abuf.at[g, r], s1_l.at[g])
        wait_for(abuf.at[g, pl.ds(0, NR - 1)], s1_r.at[g])
        pltpu.make_async_copy(abuf.at[g, z, :, yh], nbuf.at[span, r, zy, core], s2_l.at[g]).start()

        @pl.loop(1, 2 * NZ)
        def _(i):
            t = zy_peer(i)
            send(
                abuf.at[g, t // 2, :, lax.rem(t, 2)], nbuf.at[span, r, zy, core],
                s2_s.at[g], s2_r.at[g], at_zy(t),
            )

    right = {"row": lax.rem(x + 1, 4) * 2 + yl, "col": c}
    left = {"row": lax.rem(x + 3, 4) * 2 + yl, "col": c}
    other = x * 2 + 1 - yl
    twin = {"row": other, "col": c}
    xl, xr, xo = lax.rem(x + 3, 4), lax.rem(x + 1, 4), lax.rem(x + 2, 4)
    way = 1 - 2 * core
    onward = at_zy(lax.rem(z + way + NZ, NZ) * 2 + yh)

    def block(s, p):
        return nbuf.at[s, p, :, core]

    def two(s, p):
        return nbuf.at[s, pl.ds(p, 2), :, core]

    def share(s, part):
        send(part, part, sh_s.at[s], sh_r.at[s], mate)

    def relay_one(s):
        @pl.when(lax.rem(s, group) == 0)
        def _():
            g = s // group
            wait_for(nbuf.at[pl.ds(0, group), r, zy, core], s2_l.at[g])
            wait_for(nbuf.at[pl.ds(0, group), r, pl.ds(0, 2 * NZ - 1), core], s2_r.at[g])
        mine = block(s, r)
        send(mine, mine, c1_s.at[s], c1_r.at[s], twin)
        send(mine, mine, c2_s.at[s, 0], c2_r.at[s, 0], right)
        send(mine, mine, c2_s.at[s, 1], c2_r.at[s, 1], left)
        share(s, mine)

    def relay_two(s):
        wait_for(block(s, r), c1_r.at[s])
        theirs = block(s, other)
        send(theirs, theirs, c2_s.at[s, 0], c2_r.at[s, 0], right)
        send(theirs, theirs, c2_s.at[s, 1], c2_r.at[s, 1], left)
        share(s, theirs)

    def relay_three(s):
        wait_for(two(s, 0), c2_r.at[s, 0])
        send(block(s, 2 * xl), block(s, 2 * xl), c3_s.at[s, 0], c3_r.at[s, 0], right)
        share(s, two(s, 2 * xl))
        wait_for(two(s, 0), c2_r.at[s, 1])
        send(block(s, 2 * xr + 1), block(s, 2 * xr + 1), c3_s.at[s, 1], c3_r.at[s, 1], left)
        share(s, two(s, 2 * xr))

    def relay_four(s):
        wait_for(block(s, r), c3_r.at[s, 0])
        wait_for(block(s, r), c3_r.at[s, 1])
        share(s, two(s, 2 * xo))

    def multiply(s):
        wait_for(nbuf.at[s, :, :, 1 - core], sh_r.at[s])
        for j in range(4):
            for h in range(2):
                high, low = halves(nbuf[s, 2 * j + h].reshape(width, lane))
                nhi[j * width:(j + 1) * width, h * lane:(h + 1) * lane] = high
                nlo[j * width:(j + 1) * width, h * lane:(h + 1) * lane] = low

        @pl.loop(0, CAP // 2)
        def _(m):
            one, two = ids[s, 2 * m], ids[s, 2 * m + 1]
            high = jnp.concatenate([ahi[one], ahi[two]], axis=0)
            low = jnp.concatenate([alo[one], alo[two]], axis=0)
            total = jnp.dot(high, nhi[...], preferred_element_type=F32)
            total += jnp.dot(high, nlo[...], preferred_element_type=F32)
            total += jnp.dot(low, nhi[...], preferred_element_type=F32)
            rows = ahi.shape[1]
            ybuf[s, :, 2 * m] = total[:rows].reshape(NZ, 2, sub, width)
            ybuf[s, :, 2 * m + 1] = total[rows:].reshape(NZ, 2, sub, width)
        b = lax.rem(z - way + NZ, NZ)
        send(ybuf.at[s, b], rbuf.at[s, 0], ring_s.at[s, 0], ring_r.at[s, 0], onward)
        send(nboth.at[s, 0], nboth.at[s, 1], n_s.at[s], n_r.at[s], across)

    def ring(s, t):
        wait_for(rbuf.at[s, t], ring_r.at[s, t])
        b = lax.rem(z - way * (t + 2) + 2 * NZ, NZ)
        ybuf[s, b] = ybuf[s, b] + rbuf[s, t]

        @pl.when(t < NZ - 2)
        def _():
            send(ybuf.at[s, b], rbuf.at[s, t + 1], ring_s.at[s, t + 1], ring_r.at[s, t + 1], onward)

        @pl.when(t == NZ - 2)
        def _():
            send(ybuf.at[s, z, :, 1 - yh], pbuf.at[s], p_s.at[s], p_r.at[s], across)
            wait_for(nboth.at[s, 1], n_r.at[s])
            for k in range(slots):
                scale = mask[s, k].astype(F32)
                fexp[k * sub:(k + 1) * sub, :] = ybuf[s, z, pos[s, k], yh] * scale
                fexp[flat + k * sub:flat + (k + 1) * sub, :] = ybuf[s, z, pos[s, k], 1 - yh] * scale
            part = lax.dot_general(
                nboth[s].reshape(2 * flat, width), fexp[...], (((0,), (0,)), ((), ())),
                precision=HIGHEST, preferred_element_type=F32,
            )
            for h in range(2):
                dbuf[s, :, h] = part[:, h * lane:(h + 1) * lane].reshape(NR, 4, sub, lane)
            drow[s, rc] = dbuf[s, r, core]

            @pl.loop(1, 2 * NR)
            def _(i):
                p = rc_peer(i)
                send(dbuf.at[s, p // 2, lax.rem(p, 2)], drow.at[s, rc], d_s.at[s, 0], d_r.at[s, 0], at_rc(p))

    def finish(s):
        wait_for(pbuf.at[s], p_r.at[s])
        yfin[...] = ybuf[s, z, :, yh] + pbuf[s]
        for k in range(slots):
            off[s, k] = yfin[pos[s, k]] * (-mask[s, k].astype(F32))

    def diag_z(s):
        wait_for(drow.at[s, pl.ds(0, 2 * NR - 1)], d_r.at[s, 0])
        ebuf[s] = jnp.sum(drow[s], axis=0)
        ez[s, zy] = ebuf[s, lax.rem(z, 4)]

        @pl.loop(1, 2 * NZ)
        def _(i):
            t = zy_peer(i)
            send(ebuf.at[s, lax.rem(t // 2, 4)], ez.at[s, zy], d_s.at[s, 1], d_r.at[s, 1], at_zy(t))

    def spread_z(s):
        wait_for(ez.at[s, pl.ds(0, 2 * NZ - 1)], d_r.at[s, 1])
        u = lax.rem(z, 4)
        gr[s, rc, u] = jnp.sum(ez[s], axis=0)
        for i in range(1, 4):
            t = (z // 4) * 4 + lax.rem(z + i, 4)
            send(gr.at[s, rc, u], gr.at[s, rc, u], d_s.at[s, 2], d_r.at[s, 2], at_zy(t * 2 + yh))

    def spread_row(s):
        wait_for(gr.at[s, rc, pl.ds(0, 3)], d_r.at[s, 2])

        @pl.loop(1, 2 * NR)
        def _(i):
            send(gr.at[s, rc], gr.at[s, rc], d_s.at[s, 3], d_r.at[s, 3], at_rc(rc_peer(i)))

    def gather_diag(s):
        wait_for(gr.at[s, pl.ds(0, 2 * NR - 1)], d_r.at[s, 3])
        whole = gr[s].reshape(NR, 2, 4, sub, lane)
        for h in range(2):
            here = slice(h * lane, (h + 1) * lane)
            diag[s, :, here] = lead[s, :, here] + whole[:, h].reshape(width, lane)

    def leading(s):
        lead[s] = lax.dot_general(
            dinv[s], dinv[s], (((0,), (0,)), ((), ())),
            precision=HIGHEST, preferred_element_type=F32,
        )

    last = LAG + NZ - 1
    stages = (
        (last + 4, gather_diag), (last + 3, spread_row), (last + 2, spread_z), (last + 1, diag_z),
        None,
        (3, relay_four), (2, relay_three), (1, relay_two), (0, relay_one),
        (LAG, multiply), (last + 1, finish), (LAG + 1, leading),
    )

    @pl.loop(0, nodes + last + 4)
    def _(n):
        for entry in stages:
            if entry is None:
                @pl.loop(0, NZ - 1)
                def _(i):
                    t = NZ - 2 - i
                    s = n - (LAG + 1) - t

                    @pl.when((s >= 0) & (s < nodes))
                    def _():
                        ring(s, t)
            else:
                lag, work = entry
                s = n - lag

                @pl.when((s >= 0) & (s < nodes))
                def _():
                    work(s)

        @pl.when(n == LAG - 1)
        def _():
            wait_for(af.at[core], a_sem.at[0])
            wait_for(af.at[1 - core], a_sem.at[2])

            @pl.loop(0, slots)
            def _(k):
                for h in range(2):
                    rows, cols = ahi.shape[1], ahi.shape[2] // 2
                    high, low = halves(af[h, k].reshape(rows, cols))
                    ahi[k, :, h * cols:(h + 1) * cols] = high
                    alo[k, :, h * cols:(h + 1) * cols] = low

    wait_for(af.at[core], a_sem.at[1])
    for g in range(groups):
        wait_for(abuf.at[g, pl.ds(0, NR - 1)], s1_s.at[g])
        wait_for(nbuf.at[pl.ds(0, group), r, pl.ds(0, 2 * NZ - 1), core], s2_s.at[g])

    @pl.loop(0, nodes)
    def _(s):
        wait_for(block(s, r), c1_s.at[s])
        for w in range(2):
            wait_for(two(s, 0), c2_s.at[s, w])
            wait_for(block(s, r), c3_s.at[s, w])
        wait_for(nbuf.at[s, :, :, core], sh_s.at[s])
        wait_for(nboth.at[s, 0], n_s.at[s])

        @pl.loop(0, NZ - 1)
        def _(t):
            wait_for(rbuf.at[s, t], ring_s.at[s, t])

        wait_for(pbuf.at[s], p_s.at[s])
        wait_for(drow.at[s, pl.ds(0, 2 * NR - 1)], d_s.at[s, 0])
        wait_for(ez.at[s, pl.ds(0, 2 * NZ - 1)], d_s.at[s, 1])
        wait_for(gr.at[s, rc, pl.ds(0, 3)], d_s.at[s, 2])
        wait_for(gr.at[s, pl.ds(0, 2 * NR - 1)], d_s.at[s, 3])


def body(ancestor_inverse, panel, diag_inverse, structure, block_slot):
    nodes, slots, sub, width = panel.shape
    group = 2 if nodes % 2 == 0 else 1
    groups = nodes // group
    lane = width // 2
    flat = slots * sub
    blocks = ancestor_inverse.reshape(slots, 2 * NZ, 2, sub, 2 * width)
    rows, depth = width // 2, 4 * width
    vmem = pl.BlockSpec(memory_space=pltpu.VMEM)
    smem = pl.BlockSpec(memory_space=pltpu.SMEM)
    hbm = pl.BlockSpec(memory_space=pl.ANY)
    dma = pltpu.SemaphoreType.DMA
    return pl.pallas_call(
        functools.partial(kernel, group),
        out_shape=(
            jax.ShapeDtypeStruct((nodes, slots, sub, width), F32),
            jax.ShapeDtypeStruct((nodes, width, width), F32),
        ),
        in_specs=[smem, smem, hbm, hbm, hbm],
        out_specs=(vmem, vmem),
        scratch_shapes=[
            pltpu.SMEM((nodes, CAP), jnp.int32),
            pltpu.SMEM((nodes, slots), jnp.int32),
            pltpu.SMEM((nodes, slots), jnp.int32),
            pltpu.VMEM((nodes, slots, sub, width), F32),
            pltpu.VMEM((nodes, width, width), F32),
            pltpu.VMEM((2, slots, 2 * NZ, sub, 2 * width), F32),
            pltpu.VMEM((slots, rows, depth), BF16),
            pltpu.VMEM((slots, rows, depth), BF16),
            pltpu.VMEM((nodes, 2, NR, sub, lane), F32),
            pltpu.VMEM((nodes, 2, flat, width), F32),
            pltpu.VMEM((groups, NR, group, 2, sub, lane), F32),
            pltpu.VMEM((nodes, NR, 2 * NZ, 2, sub, lane), F32),
            pltpu.VMEM((depth, width), BF16),
            pltpu.VMEM((depth, width), BF16),
            pltpu.VMEM((nodes, NZ, CAP, 2, sub, width), F32),
            pltpu.VMEM((nodes, NZ - 1, CAP, 2, sub, width), F32),
            pltpu.VMEM((nodes, CAP, sub, width), F32),
            pltpu.VMEM((CAP, sub, width), F32),
            pltpu.VMEM((2 * flat, width), F32),
            pltpu.VMEM((nodes, NR, 2, 4, sub, lane), F32),
            pltpu.VMEM((nodes, 2 * NR, 4, sub, lane), F32),
            pltpu.VMEM((nodes, 4, sub, lane), F32),
            pltpu.VMEM((nodes, 2 * NZ, sub, lane), F32),
            pltpu.VMEM((nodes, 2 * NR, 4, sub, lane), F32),
            pltpu.VMEM((nodes, width, width), F32),
            dma((2,)), dma((3,)),
            dma((groups,)), dma((groups,)), dma((groups,)),
            dma((groups,)), dma((groups,)), dma((groups,)),
            dma((nodes,)), dma((nodes,)),
            dma((nodes, 2)), dma((nodes, 2)),
            dma((nodes, 2)), dma((nodes, 2)),
            dma((nodes,)), dma((nodes,)),
            dma((nodes,)), dma((nodes,)),
            dma((nodes, NZ - 1)), dma((nodes, NZ - 1)),
            dma((nodes,)), dma((nodes,)),
            dma((nodes, 4)), dma((nodes, 4)),
        ],
        compiler_params=pltpu.CompilerParams(
            collective_id=0, has_side_effects=True, vmem_limit_bytes=62 * 1024 * 1024
        ),
        name="invert_level",
    )(structure, block_slot, blocks, panel, diag_inverse)


def solution(mesh):
    in_specs = (P("row", "col"), P(None, "row", "col", None), P(), P(), P())
    out_specs = (P(None, "row", "col", None), P())
    return jax.shard_map(body, mesh=mesh, in_specs=in_specs, out_specs=out_specs, check_vma=False)
```

```python
import functools

import jax
import jax.numpy as jnp
from jax import lax
from jax.experimental import pallas as pl
from jax.experimental.pallas import tpu as pltpu
from jax.sharding import PartitionSpec as P

F32 = jnp.float32
BF16 = jnp.bfloat16
MESH = pl.DeviceIdType.MESH
HIGHEST = lax.Precision.HIGHEST

NR = 8
NZ = 8
CAP = 6
LAG = 3


def halves(value):
    high = value.astype(BF16)
    return high, (value - high.astype(F32)).astype(BF16)


def wait_for(ref, sem):
    pltpu.make_async_copy(ref, ref, sem).wait()


def kernel(
    group,
    structure, place, a_ref, panel_ref, dinv_ref, off, diag,
    bits, ids, pos, mask, panel, dinv,
    af, ahi, alo, nsrc, nboth, abuf, nbuf, nhi, nlo, ybuf, rbuf, pbuf, yfin, fexp,
    dbuf, drow, ebuf, ez, gr, lead,
    in_sem, a_sem, s1_s, s1_r, s1_l, s2_s, s2_r, s2_l,
    c1_s, c1_r, c2_s, c2_r, c3_s, c3_r, sh_s, sh_r, n_s, n_r,
    ring_s, ring_r, p_s, p_r, d_s, d_r,
):
    nodes, slots, sub, width = panel.shape
    lane = width // 2
    flat = slots * sub
    groups = nodes // group
    r = lax.axis_index("row")
    c = lax.axis_index("col")
    z = c // 4
    yh = lax.rem(c // 2, 2)
    core = lax.rem(c, 2)
    zy = c // 2
    rc = r * 2 + core
    x = r // 2
    yl = lax.rem(r, 2)

    def send(src, dst, ssem, rsem, where):
        pltpu.make_async_remote_copy(
            src_ref=src, dst_ref=dst, send_sem=ssem, recv_sem=rsem,
            device_id=where, device_id_type=MESH,
        ).start()

    def at_rc(t):
        return {"row": t // 2, "col": zy * 2 + lax.rem(t, 2)}

    def at_zy(t):
        return {"row": r, "col": t * 2 + core}

    def rc_peer(i):
        return lax.rem(rc + i, 2 * NR)

    def zy_peer(i):
        return lax.rem(zy + i, 2 * NZ)

    mate = {"row": r, "col": zy * 2 + 1 - core}
    across = at_zy(z * 2 + 1 - yh)

    load_panel = pltpu.make_async_copy(panel_ref, panel, in_sem.at[0])
    load_dinv = pltpu.make_async_copy(dinv_ref, dinv, in_sem.at[1])
    own_a = pltpu.make_async_copy(a_ref.at[:, :, core], af.at[core], a_sem.at[0])
    load_panel.start()
    load_dinv.start()
    own_a.start()

    barrier = pltpu.get_barrier_semaphore()

    @pl.loop(1, 2 * NR)
    def _(i):
        pl.semaphore_signal(barrier, inc=1, device_id=at_rc(rc_peer(i)), device_id_type=MESH)
        pl.semaphore_signal(barrier, inc=1, device_id=at_zy(zy_peer(i)), device_id_type=MESH)

    @pl.loop(0, place.shape[0])
    def _(b):
        slot = place[b] - r * slots
        bits[b] = sum((slot == i).astype(jnp.int32) * (1 << i) for i in range(slots))

    @pl.loop(0, nodes)
    def _(s):
        used = bits[structure[s, 0]]
        for k in range(1, structure.shape[1]):
            used = used + bits[structure[s, k]]
        seen = [lax.shift_right_logical(used, jnp.int32(i)) & 1 for i in range(slots)]
        before = jnp.int32(0)
        spots = []
        for i in range(slots):
            mask[s, i] = seen[i]
            pos[s, i] = before * seen[i]
            spots.append(before)
            before = before + seen[i]
        for k in range(CAP):
            found = jnp.int32(0)
            for i in range(slots):
                found = found + i * seen[i] * (spots[i] == k).astype(jnp.int32)
            ids[s, k] = found

    load_panel.wait()
    load_dinv.wait()

    @pl.loop(0, nodes)
    def _(s):
        value = jnp.dot(
            panel[s].reshape(flat, width), dinv[s],
            precision=HIGHEST, preferred_element_type=F32,
        )
        for k in range(slots):
            part = value[k * sub:(k + 1) * sub] * mask[s, k].astype(F32)
            nboth[s, 0, k * sub:(k + 1) * sub, :] = part
            for h in range(2):
                nsrc[s, k // 4, (k % 4) * 2 + h] = part[:, h * lane:(h + 1) * lane]

    pl.semaphore_wait(barrier, 2 * (2 * NR - 1))

    def exchange_row(g):
        span = pl.ds(g * group, group)
        pltpu.make_async_copy(nsrc.at[span, :, r], abuf.at[g, r], s1_l.at[g]).start()

        @pl.loop(1, NR)
        def _(i):
            p = lax.rem(r + i, NR)
            send(nsrc.at[span, :, p], abuf.at[g, r], s1_s.at[g], s1_r.at[g], {"row": p, "col": c})

    def exchange_col(g):
        span = pl.ds(g * group, group)
        wait_for(abuf.at[g, r], s1_l.at[g])
        wait_for(abuf.at[g, pl.ds(0, NR - 1)], s1_r.at[g])
        pltpu.make_async_copy(abuf.at[g, z, :, yh], nbuf.at[span, r, zy, core], s2_l.at[g]).start()

        @pl.loop(1, 2 * NZ)
        def _(i):
            t = zy_peer(i)
            send(
                abuf.at[g, t // 2, :, lax.rem(t, 2)], nbuf.at[span, r, zy, core],
                s2_s.at[g], s2_r.at[g], at_zy(t),
            )

    exchange_row(0)
    exchange_row(1)
    send(a_ref.at[:, :, 1 - core], af.at[core], a_sem.at[1], a_sem.at[2], mate)
    exchange_col(0)

    @pl.loop(2, groups)
    def _(g):
        exchange_row(g)

    exchange_col(1)

    right = {"row": lax.rem(x + 1, 4) * 2 + yl, "col": c}
    left = {"row": lax.rem(x + 3, 4) * 2 + yl, "col": c}
    other = x * 2 + 1 - yl
    twin = {"row": other, "col": c}
    xl, xr, xo = lax.rem(x + 3, 4), lax.rem(x + 1, 4), lax.rem(x + 2, 4)
    way = 1 - 2 * core
    onward = at_zy(lax.rem(z + way + NZ, NZ) * 2 + yh)

    def block(s, p):
        return nbuf.at[s, p, :, core]

    def two(s, p):
        return nbuf.at[s, pl.ds(p, 2), :, core]

    def share(s, part):
        send(part, part, sh_s.at[s], sh_r.at[s], mate)

    def relay_one(s):
        wait_for(nbuf.at[pl.ds(0, group), r, zy, core], s2_l.at[s])
        wait_for(nbuf.at[pl.ds(0, group), r, pl.ds(0, 2 * NZ - 1), core], s2_r.at[s])

        @pl.when(s + 2 < groups)
        def _():
            exchange_col(s + 2)

        mine = block(s, r)
        send(mine, mine, c1_s.at[s], c1_r.at[s], twin)
        send(mine, mine, c2_s.at[s, 0], c2_r.at[s, 0], right)
        send(mine, mine, c2_s.at[s, 1], c2_r.at[s, 1], left)
        share(s, mine)

    def relay_two(s):
        wait_for(block(s, r), c1_r.at[s])
        theirs = block(s, other)
        send(theirs, theirs, c2_s.at[s, 0], c2_r.at[s, 0], right)
        send(theirs, theirs, c2_s.at[s, 1], c2_r.at[s, 1], left)
        share(s, theirs)

    def relay_three(s):
        wait_for(two(s, 0), c2_r.at[s, 0])
        send(block(s, 2 * xl), block(s, 2 * xl), c3_s.at[s, 0], c3_r.at[s, 0], right)
        share(s, two(s, 2 * xl))
        wait_for(two(s, 0), c2_r.at[s, 1])
        send(block(s, 2 * xr + 1), block(s, 2 * xr + 1), c3_s.at[s, 1], c3_r.at[s, 1], left)
        share(s, two(s, 2 * xr))

    def relay_four(s):
        wait_for(block(s, r), c3_r.at[s, 0])
        wait_for(block(s, r), c3_r.at[s, 1])
        share(s, two(s, 2 * xo))

    def multiply(s):
        wait_for(nbuf.at[s, :, :, 1 - core], sh_r.at[s])
        for j in range(4):
            for h in range(2):
                high, low = halves(nbuf[s, 2 * j + h].reshape(width, lane))
                nhi[j * width:(j + 1) * width, h * lane:(h + 1) * lane] = high
                nlo[j * width:(j + 1) * width, h * lane:(h + 1) * lane] = low

        @pl.loop(0, CAP // 2)
        def _(m):
            one, two = ids[s, 2 * m], ids[s, 2 * m + 1]
            high = jnp.concatenate([ahi[one], ahi[two]], axis=0)
            low = jnp.concatenate([alo[one], alo[two]], axis=0)
            total = jnp.dot(high, nhi[...], preferred_element_type=F32)
            total += jnp.dot(high, nlo[...], preferred_element_type=F32)
            total += jnp.dot(low, nhi[...], preferred_element_type=F32)
            rows = ahi.shape[1]
            ybuf[s, :, 2 * m] = total[:rows].reshape(NZ, 2, sub, width)
            ybuf[s, :, 2 * m + 1] = total[rows:].reshape(NZ, 2, sub, width)
        b = lax.rem(z - way + NZ, NZ)
        send(ybuf.at[s, b], rbuf.at[s, 0], ring_s.at[s, 0], ring_r.at[s, 0], onward)
        send(nboth.at[s, 0], nboth.at[s, 1], n_s.at[s], n_r.at[s], across)

    def ring(s, t):
        wait_for(rbuf.at[s, t], ring_r.at[s, t])
        b = lax.rem(z - way * (t + 2) + 2 * NZ, NZ)
        ybuf[s, b] = ybuf[s, b] + rbuf[s, t]

        @pl.when(t < NZ - 2)
        def _():
            send(ybuf.at[s, b], rbuf.at[s, t + 1], ring_s.at[s, t + 1], ring_r.at[s, t + 1], onward)

        @pl.when(t == NZ - 2)
        def _():
            send(ybuf.at[s, z, :, 1 - yh], pbuf.at[s], p_s.at[s], p_r.at[s], across)
            wait_for(nboth.at[s, 1], n_r.at[s])
            for k in range(slots):
                scale = mask[s, k].astype(F32)
                fexp[k * sub:(k + 1) * sub, :] = ybuf[s, z, pos[s, k], yh] * scale
                fexp[flat + k * sub:flat + (k + 1) * sub, :] = ybuf[s, z, pos[s, k], 1 - yh] * scale
            part = lax.dot_general(
                nboth[s].reshape(2 * flat, width), fexp[...], (((0,), (0,)), ((), ())),
                precision=HIGHEST, preferred_element_type=F32,
            )
            for h in range(2):
                dbuf[s, :, h] = part[:, h * lane:(h + 1) * lane].reshape(NR, 4, sub, lane)
            drow[s, rc] = dbuf[s, r, core]

            @pl.loop(1, 2 * NR)
            def _(i):
                p = rc_peer(i)
                send(dbuf.at[s, p // 2, lax.rem(p, 2)], drow.at[s, rc], d_s.at[s, 0], d_r.at[s, 0], at_rc(p))

    def finish(s):
        wait_for(pbuf.at[s], p_r.at[s])
        yfin[...] = ybuf[s, z, :, yh] + pbuf[s]
        for k in range(slots):
            off[s, k] = yfin[pos[s, k]] * (-mask[s, k].astype(F32))

    def diag_z(s):
        wait_for(drow.at[s, pl.ds(0, 2 * NR - 1)], d_r.at[s, 0])
        ebuf[s] = jnp.sum(drow[s], axis=0)
        ez[s, zy] = ebuf[s, lax.rem(z, 4)]

        @pl.loop(1, 2 * NZ)
        def _(i):
            t = zy_peer(i)
            send(ebuf.at[s, lax.rem(t // 2, 4)], ez.at[s, zy], d_s.at[s, 1], d_r.at[s, 1], at_zy(t))

    def spread_z(s):
        wait_for(ez.at[s, pl.ds(0, 2 * NZ - 1)], d_r.at[s, 1])
        u = lax.rem(z, 4)
        gr[s, rc, u] = jnp.sum(ez[s], axis=0)
        for i in range(1, 4):
            t = (z // 4) * 4 + lax.rem(z + i, 4)
            send(gr.at[s, rc, u], gr.at[s, rc, u], d_s.at[s, 2], d_r.at[s, 2], at_zy(t * 2 + yh))

    def spread_row(s):
        wait_for(gr.at[s, rc, pl.ds(0, 3)], d_r.at[s, 2])

        @pl.loop(1, 2 * NR)
        def _(i):
            send(gr.at[s, rc], gr.at[s, rc], d_s.at[s, 3], d_r.at[s, 3], at_rc(rc_peer(i)))

    def gather_diag(s):
        wait_for(gr.at[s, pl.ds(0, 2 * NR - 1)], d_r.at[s, 3])
        whole = gr[s].reshape(NR, 2, 4, sub, lane)
        for h in range(2):
            here = slice(h * lane, (h + 1) * lane)
            diag[s, :, here] = lead[s, :, here] + whole[:, h].reshape(width, lane)

    def leading(s):
        lead[s] = lax.dot_general(
            dinv[s], dinv[s], (((0,), (0,)), ((), ())),
            precision=HIGHEST, preferred_element_type=F32,
        )

    last = LAG + NZ - 1
    stages = (
        None,
        (3, relay_four), (LAG, multiply), (2, relay_three), (1, relay_two), (0, relay_one),
        (last + 8, gather_diag), (last + 6, spread_row), (last + 4, spread_z), (last + 2, diag_z),
        (last + 3, finish), (LAG + 1, leading),
    )

    @pl.loop(0, nodes + last + 8)
    def _(n):
        for entry in stages:
            if entry is None:
                @pl.loop(0, NZ - 1)
                def _(i):
                    t = NZ - 2 - i
                    s = n - (LAG + 1) - t

                    @pl.when((s >= 0) & (s < nodes))
                    def _():
                        ring(s, t)
            else:
                lag, work = entry
                s = n - lag

                @pl.when((s >= 0) & (s < nodes))
                def _():
                    work(s)

        @pl.when(n == LAG - 1)
        def _():
            wait_for(af.at[core], a_sem.at[0])
            wait_for(af.at[1 - core], a_sem.at[2])

            @pl.loop(0, slots)
            def _(k):
                for h in range(2):
                    rows, cols = ahi.shape[1], ahi.shape[2] // 2
                    high, low = halves(af[h, k].reshape(rows, cols))
                    ahi[k, :, h * cols:(h + 1) * cols] = high
                    alo[k, :, h * cols:(h + 1) * cols] = low

    wait_for(af.at[core], a_sem.at[1])
    for g in range(groups):
        wait_for(abuf.at[g, pl.ds(0, NR - 1)], s1_s.at[g])
        wait_for(nbuf.at[pl.ds(0, group), r, pl.ds(0, 2 * NZ - 1), core], s2_s.at[g])

    @pl.loop(0, nodes)
    def _(s):
        wait_for(block(s, r), c1_s.at[s])
        for w in range(2):
            wait_for(two(s, 0), c2_s.at[s, w])
            wait_for(block(s, r), c3_s.at[s, w])
        wait_for(nbuf.at[s, :, :, core], sh_s.at[s])
        wait_for(nboth.at[s, 0], n_s.at[s])

        @pl.loop(0, NZ - 1)
        def _(t):
            wait_for(rbuf.at[s, t], ring_s.at[s, t])

        wait_for(pbuf.at[s], p_s.at[s])
        wait_for(drow.at[s, pl.ds(0, 2 * NR - 1)], d_s.at[s, 0])
        wait_for(ez.at[s, pl.ds(0, 2 * NZ - 1)], d_s.at[s, 1])
        wait_for(gr.at[s, rc, pl.ds(0, 3)], d_s.at[s, 2])
        wait_for(gr.at[s, pl.ds(0, 2 * NR - 1)], d_s.at[s, 3])


def body(ancestor_inverse, panel, diag_inverse, structure, block_slot):
    nodes, slots, sub, width = panel.shape
    group = 1
    groups = nodes // group
    lane = width // 2
    flat = slots * sub
    blocks = ancestor_inverse.reshape(slots, 2 * NZ, 2, sub, 2 * width)
    rows, depth = width // 2, 4 * width
    vmem = pl.BlockSpec(memory_space=pltpu.VMEM)
    smem = pl.BlockSpec(memory_space=pltpu.SMEM)
    hbm = pl.BlockSpec(memory_space=pl.ANY)
    dma = pltpu.SemaphoreType.DMA
    return pl.pallas_call(
        functools.partial(kernel, group),
        out_shape=(
            jax.ShapeDtypeStruct((nodes, slots, sub, width), F32),
            jax.ShapeDtypeStruct((nodes, width, width), F32),
        ),
        in_specs=[smem, smem, hbm, hbm, hbm],
        out_specs=(vmem, vmem),
        scratch_shapes=[
            pltpu.SMEM(block_slot.shape, jnp.int32),
            pltpu.SMEM((nodes, CAP), jnp.int32),
            pltpu.SMEM((nodes, slots), jnp.int32),
            pltpu.SMEM((nodes, slots), jnp.int32),
            pltpu.VMEM((nodes, slots, sub, width), F32),
            pltpu.VMEM((nodes, width, width), F32),
            pltpu.VMEM((2, slots, 2 * NZ, sub, 2 * width), F32),
            pltpu.VMEM((slots, rows, depth), BF16),
            pltpu.VMEM((slots, rows, depth), BF16),
            pltpu.VMEM((nodes, 2, NR, sub, lane), F32),
            pltpu.VMEM((nodes, 2, flat, width), F32),
            pltpu.VMEM((groups, NR, group, 2, sub, lane), F32),
            pltpu.VMEM((nodes, NR, 2 * NZ, 2, sub, lane), F32),
            pltpu.VMEM((depth, width), BF16),
            pltpu.VMEM((depth, width), BF16),
            pltpu.VMEM((nodes, NZ, CAP, 2, sub, width), F32),
            pltpu.VMEM((nodes, NZ - 1, CAP, 2, sub, width), F32),
            pltpu.VMEM((nodes, CAP, sub, width), F32),
            pltpu.VMEM((CAP, sub, width), F32),
            pltpu.VMEM((2 * flat, width), F32),
            pltpu.VMEM((nodes, NR, 2, 4, sub, lane), F32),
            pltpu.VMEM((nodes, 2 * NR, 4, sub, lane), F32),
            pltpu.VMEM((nodes, 4, sub, lane), F32),
            pltpu.VMEM((nodes, 2 * NZ, sub, lane), F32),
            pltpu.VMEM((nodes, 2 * NR, 4, sub, lane), F32),
            pltpu.VMEM((nodes, width, width), F32),
            dma((2,)), dma((3,)),
            dma((groups,)), dma((groups,)), dma((groups,)),
            dma((groups,)), dma((groups,)), dma((groups,)),
            dma((nodes,)), dma((nodes,)),
            dma((nodes, 2)), dma((nodes, 2)),
            dma((nodes, 2)), dma((nodes, 2)),
            dma((nodes,)), dma((nodes,)),
            dma((nodes,)), dma((nodes,)),
            dma((nodes, NZ - 1)), dma((nodes, NZ - 1)),
            dma((nodes,)), dma((nodes,)),
            dma((nodes, 4)), dma((nodes, 4)),
        ],
        compiler_params=pltpu.CompilerParams(
            collective_id=0, has_side_effects=True, vmem_limit_bytes=62 * 1024 * 1024
        ),
        name="invert_level",
    )(structure, block_slot, blocks, panel, diag_inverse)


def solution(mesh):
    in_specs = (P("row", "col"), P(None, "row", "col", None), P(), P(), P())
    out_specs = (P(None, "row", "col", None), P())
    return jax.shard_map(body, mesh=mesh, in_specs=in_specs, out_specs=out_specs, check_vma=False)
```

```python
import functools

import jax
import jax.numpy as jnp
from jax import lax
from jax.experimental import pallas as pl
from jax.experimental.pallas import tpu as pltpu
from jax.sharding import PartitionSpec as P

F32 = jnp.float32
BF16 = jnp.bfloat16
MESH = pl.DeviceIdType.MESH
HIGHEST = lax.Precision.HIGHEST

NR = 8
NZ = 8
CAP = 6
LAG = 3


def halves(value):
    high = value.astype(BF16)
    return high, (value - high.astype(F32)).astype(BF16)


def wait_for(ref, sem):
    pltpu.make_async_copy(ref, ref, sem).wait()


def kernel(
    group,
    structure, place, a_ref, panel_ref, dinv_ref, off_ref, diag_ref,
    off, diag, bits, ids, pos, mask, panel, dinv,
    af, ahi, alo, nsrc, nboth, abuf, nbuf, nhi, nlo, ybuf, rbuf, pbuf, yfin, fexp,
    dbuf, dmate, dsum, drow, ebuf, ez, gr, lead,
    in_sem, o_sem, a_sem, s1_s, s1_r, s1_l, s2_s, s2_r, s2_l,
    c1_s, c1_r, c2_s, c2_r, c3_s, c3_r, sh_s, sh_r, n_s, n_r,
    ring_s, ring_r, p_s, p_r, d_s, d_r,
):
    nodes, slots, sub, width = panel.shape
    lane = width // 2
    flat = slots * sub
    groups = nodes // group
    r = lax.axis_index("row")
    c = lax.axis_index("col")
    z = c // 4
    yh = lax.rem(c // 2, 2)
    core = lax.rem(c, 2)
    zy = c // 2
    x = r // 2
    yl = lax.rem(r, 2)

    def send(src, dst, ssem, rsem, where):
        pltpu.make_async_remote_copy(
            src_ref=src, dst_ref=dst, send_sem=ssem, recv_sem=rsem,
            device_id=where, device_id_type=MESH,
        ).start()

    def at_row(t):
        return {"row": t, "col": c}

    def at_zy(t):
        return {"row": r, "col": t * 2 + core}

    def row_peer(i):
        return lax.rem(r + i, NR)

    def zy_peer(i):
        return lax.rem(zy + i, 2 * NZ)

    mate = {"row": r, "col": zy * 2 + 1 - core}
    across = at_zy(z * 2 + 1 - yh)

    load_panel = pltpu.make_async_copy(panel_ref, panel, in_sem.at[0])
    load_dinv = pltpu.make_async_copy(dinv_ref, dinv, in_sem.at[1])
    own_a = pltpu.make_async_copy(a_ref.at[:, :, core], af.at[core], a_sem.at[0])
    load_panel.start()
    load_dinv.start()
    own_a.start()

    barrier = pltpu.get_barrier_semaphore()

    def greet(where):
        pl.semaphore_signal(barrier, inc=1, device_id=where, device_id_type=MESH)

    @pl.loop(1, 2 * NZ)
    def _(i):
        greet(at_zy(zy_peer(i)))

    @pl.loop(1, NR)
    def _(i):
        greet(at_row(row_peer(i)))

    greet(mate)

    @pl.loop(0, place.shape[0])
    def _(b):
        slot = place[b] - r * slots
        bits[b] = sum((slot == i).astype(jnp.int32) * (1 << i) for i in range(slots))

    @pl.loop(0, nodes)
    def _(s):
        used = bits[structure[s, 0]]
        for k in range(1, structure.shape[1]):
            used = used + bits[structure[s, k]]
        seen = [lax.shift_right_logical(used, jnp.int32(i)) & 1 for i in range(slots)]
        for i in range(slots):
            mask[s, i] = seen[i]

    load_panel.wait()
    load_dinv.wait()

    @pl.loop(0, nodes)
    def _(s):
        value = jnp.dot(
            panel[s].reshape(flat, width), dinv[s],
            precision=HIGHEST, preferred_element_type=F32,
        )
        for k in range(slots):
            part = value[k * sub:(k + 1) * sub] * mask[s, k].astype(F32)
            nboth[s, 0, k * sub:(k + 1) * sub, :] = part
            for h in range(2):
                nsrc[s, k // 4, (k % 4) * 2 + h] = part[:, h * lane:(h + 1) * lane]

    pl.semaphore_wait(barrier, 2 * NZ - 1 + NR)

    def exchange_row(g):
        span = pl.ds(g * group, group)
        pltpu.make_async_copy(nsrc.at[span, :, r], abuf.at[g, r], s1_l.at[g]).start()

        @pl.loop(1, NR)
        def _(i):
            p = lax.rem(r + i, NR)
            send(nsrc.at[span, :, p], abuf.at[g, r], s1_s.at[g], s1_r.at[g], {"row": p, "col": c})

    def exchange_col(g):
        span = pl.ds(g * group, group)
        wait_for(abuf.at[g, r], s1_l.at[g])
        wait_for(abuf.at[g, pl.ds(0, NR - 1)], s1_r.at[g])
        pltpu.make_async_copy(abuf.at[g, z, :, yh], nbuf.at[span, r, zy, core], s2_l.at[g]).start()

        @pl.loop(1, 2 * NZ)
        def _(i):
            t = zy_peer(i)
            send(
                abuf.at[g, t // 2, :, lax.rem(t, 2)], nbuf.at[span, r, zy, core],
                s2_s.at[g], s2_r.at[g], at_zy(t),
            )

    exchange_row(0)
    exchange_row(1)
    send(a_ref.at[:, :, 1 - core], af.at[core], a_sem.at[1], a_sem.at[2], mate)
    exchange_col(0)

    @pl.loop(0, nodes)
    def _(s):
        before = jnp.int32(0)
        spots = []
        for i in range(slots):
            pos[s, i] = before * mask[s, i]
            spots.append(before)
            before = before + mask[s, i]
        for k in range(CAP):
            found = jnp.int32(0)
            for i in range(slots):
                found = found + i * mask[s, i] * (spots[i] == k).astype(jnp.int32)
            ids[s, k] = found

    @pl.loop(2, groups)
    def _(g):
        exchange_row(g)

    exchange_col(1)

    right = {"row": lax.rem(x + 1, 4) * 2 + yl, "col": c}
    left = {"row": lax.rem(x + 3, 4) * 2 + yl, "col": c}
    other = x * 2 + 1 - yl
    twin = {"row": other, "col": c}
    xl, xr, xo = lax.rem(x + 3, 4), lax.rem(x + 1, 4), lax.rem(x + 2, 4)
    way = 1 - 2 * core
    long_hops, short_hops = NZ // 2, NZ // 2 - 1

    def z_at(d):
        return lax.rem(z + d + NZ, NZ)

    after_long = at_zy(z_at(-way) * 2 + yh)
    after_short = at_zy(z_at(way) * 2 + yh)

    def pass_long(s, t):
        part = ybuf.at[s, z_at(-way * (long_hops - t))]
        send(part, rbuf.at[s, t], ring_s.at[s, t], ring_r.at[s, t], after_long)

    def pass_short(s, t):
        part = ybuf.at[s, z_at(way * (short_hops - t))]
        k = long_hops + t
        send(part, rbuf.at[s, k], ring_s.at[s, k], ring_r.at[s, k], after_short)

    def block(s, p):
        return nbuf.at[s, p, :, core]

    def two(s, p):
        return nbuf.at[s, pl.ds(p, 2), :, core]

    def share(s, part):
        send(part, part, sh_s.at[s], sh_r.at[s], mate)

    def relay_one(s):
        wait_for(nbuf.at[pl.ds(0, group), r, zy, core], s2_l.at[s])
        wait_for(nbuf.at[pl.ds(0, group), r, pl.ds(0, 2 * NZ - 1), core], s2_r.at[s])

        @pl.when(s + 2 < groups)
        def _():
            exchange_col(s + 2)

        mine = block(s, r)
        send(mine, mine, c1_s.at[s], c1_r.at[s], twin)
        send(mine, mine, c2_s.at[s, 0], c2_r.at[s, 0], right)
        send(mine, mine, c2_s.at[s, 1], c2_r.at[s, 1], left)
        share(s, mine)

    def relay_two(s):
        wait_for(block(s, r), c1_r.at[s])
        theirs = block(s, other)
        send(theirs, theirs, c2_s.at[s, 0], c2_r.at[s, 0], right)
        send(theirs, theirs, c2_s.at[s, 1], c2_r.at[s, 1], left)
        share(s, theirs)

    def relay_three(s):
        wait_for(two(s, 0), c2_r.at[s, 0])
        send(block(s, 2 * xl), block(s, 2 * xl), c3_s.at[s, 0], c3_r.at[s, 0], right)
        share(s, two(s, 2 * xl))
        wait_for(two(s, 0), c2_r.at[s, 1])
        send(block(s, 2 * xr + 1), block(s, 2 * xr + 1), c3_s.at[s, 1], c3_r.at[s, 1], left)
        share(s, two(s, 2 * xr))

    def relay_four(s):
        wait_for(block(s, r), c3_r.at[s, 0])
        wait_for(block(s, r), c3_r.at[s, 1])
        share(s, two(s, 2 * xo))

    def multiply(s):
        wait_for(nbuf.at[s, :, :, 1 - core], sh_r.at[s])
        for j in range(4):
            for h in range(2):
                high, low = halves(nbuf[s, 2 * j + h].reshape(width, lane))
                nhi[j * width:(j + 1) * width, h * lane:(h + 1) * lane] = high
                nlo[j * width:(j + 1) * width, h * lane:(h + 1) * lane] = low

        @pl.loop(0, CAP // 2)
        def _(m):
            one, two = ids[s, 2 * m], ids[s, 2 * m + 1]
            high = jnp.concatenate([ahi[one], ahi[two]], axis=0)
            low = jnp.concatenate([alo[one], alo[two]], axis=0)
            total = jnp.dot(high, nhi[...], preferred_element_type=F32)
            total += jnp.dot(high, nlo[...], preferred_element_type=F32)
            total += jnp.dot(low, nhi[...], preferred_element_type=F32)
            rows = ahi.shape[1]
            ybuf[s, :, 2 * m] = total[:rows].reshape(NZ, 2, sub, width)
            ybuf[s, :, 2 * m + 1] = total[rows:].reshape(NZ, 2, sub, width)
        pass_long(s, 0)
        pass_short(s, 0)
        send(nboth.at[s, 0], nboth.at[s, 1], n_s.at[s], n_r.at[s], across)

    def ring(s, t):
        wait_for(rbuf.at[s, t], ring_r.at[s, t])
        b = z_at(-way * (long_hops - 1 - t))
        ybuf[s, b] = ybuf[s, b] + rbuf[s, t]

        @pl.when(t < long_hops - 1)
        def _():
            pass_long(s, t + 1)
            k = long_hops + t
            wait_for(rbuf.at[s, k], ring_r.at[s, k])
            f = z_at(way * (short_hops - 1 - t))
            ybuf[s, f] = ybuf[s, f] + rbuf[s, k]

            @pl.when(t < short_hops - 1)
            def _():
                pass_short(s, t + 1)

        @pl.when(t == long_hops - 1)
        def _():
            send(ybuf.at[s, z, :, 1 - yh], pbuf.at[s], p_s.at[s], p_r.at[s], across)
            wait_for(nboth.at[s, 1], n_r.at[s])
            for k in range(slots):
                scale = mask[s, k].astype(F32)
                fexp[k * sub:(k + 1) * sub, :] = ybuf[s, z, pos[s, k], yh] * scale
                fexp[flat + k * sub:flat + (k + 1) * sub, :] = ybuf[s, z, pos[s, k], 1 - yh] * scale
            part = lax.dot_general(
                nboth[s].reshape(2 * flat, width), fexp[...], (((0,), (0,)), ((), ())),
                precision=HIGHEST, preferred_element_type=F32,
            )
            for h in range(2):
                dbuf[s, h] = part[:, h * lane:(h + 1) * lane].reshape(NR, 4, sub, lane)
            send(dbuf.at[s, 1 - core], dmate.at[s], d_s.at[s, 4], d_r.at[s, 4], mate)

    def diag_row(s):
        wait_for(dmate.at[s], d_r.at[s, 4])
        dsum[s] = dbuf[s, core] + dmate[s]
        drow[s, r] = dsum[s, r]

        @pl.loop(1, NR)
        def _(i):
            p = row_peer(i)
            send(dsum.at[s, p], drow.at[s, r], d_s.at[s, 0], d_r.at[s, 0], at_row(p))

    def finish(s):
        wait_for(pbuf.at[s], p_r.at[s])
        yfin[...] = ybuf[s, z, :, yh] + pbuf[s]
        for k in range(slots):
            off[s, k] = yfin[pos[s, k]] * (-mask[s, k].astype(F32))
        pltpu.make_async_copy(off.at[s], off_ref.at[s], o_sem.at[0, s]).start()

    def diag_z(s):
        wait_for(drow.at[s, pl.ds(0, NR - 1)], d_r.at[s, 0])
        ebuf[s] = jnp.sum(drow[s], axis=0)
        ez[s, zy] = ebuf[s, lax.rem(z, 4)]

        @pl.loop(1, 2 * NZ)
        def _(i):
            t = zy_peer(i)
            send(ebuf.at[s, lax.rem(t // 2, 4)], ez.at[s, zy], d_s.at[s, 1], d_r.at[s, 1], at_zy(t))

    def spread_z(s):
        wait_for(ez.at[s, pl.ds(0, 2 * NZ - 1)], d_r.at[s, 1])
        u = lax.rem(z, 4)
        here = gr.at[s, core, r, u]
        gr[s, core, r, u] = jnp.sum(ez[s], axis=0)
        for i in range(1, 4):
            t = (z // 4) * 4 + lax.rem(z + i, 4)
            send(here, here, d_s.at[s, 2], d_r.at[s, 2], at_zy(t * 2 + yh))

    def spread_row(s):
        wait_for(gr.at[s, core, r, pl.ds(0, 3)], d_r.at[s, 2])
        here = gr.at[s, core, r]

        @pl.loop(1, NR)
        def _(i):
            send(here, here, d_s.at[s, 3], d_r.at[s, 3], at_row(row_peer(i)))

    def spread_core(s):
        wait_for(gr.at[s, core, pl.ds(0, NR - 1)], d_r.at[s, 3])
        here = gr.at[s, core]
        send(here, here, d_s.at[s, 5], d_r.at[s, 5], mate)

    def gather_diag(s):
        wait_for(gr.at[s, 1 - core], d_r.at[s, 5])
        for h in range(2):
            here = slice(h * lane, (h + 1) * lane)
            diag[s, :, here] = lead[s, :, here] + gr[s, h].reshape(width, lane)
        pltpu.make_async_copy(diag.at[s], diag_ref.at[s], o_sem.at[1, s]).start()

    def leading(s):
        lead[s] = lax.dot_general(
            dinv[s], dinv[s], (((0,), (0,)), ((), ())),
            precision=HIGHEST, preferred_element_type=F32,
        )

    def settle(s):
        wait_for(abuf.at[s, pl.ds(0, NR - 1)], s1_s.at[s])
        wait_for(nbuf.at[pl.ds(0, group), r, pl.ds(0, 2 * NZ - 1), core], s2_s.at[s])
        wait_for(block(s, r), c1_s.at[s])
        for w in range(2):
            wait_for(two(s, 0), c2_s.at[s, w])
            wait_for(block(s, r), c3_s.at[s, w])
        wait_for(nbuf.at[s, :, :, core], sh_s.at[s])
        wait_for(nboth.at[s, 0], n_s.at[s])
        for t in range(NZ - 1):
            wait_for(rbuf.at[s, t], ring_s.at[s, t])
        wait_for(pbuf.at[s], p_s.at[s])

    last = LAG + long_hops
    stages = (
        (2, relay_three), (1, relay_two), (0, relay_one), (3, relay_four), (LAG, multiply),
        (last + 1, diag_row), (last + 2, diag_z), (last + 4, spread_z), (last + 5, spread_row),
        (last + 7, spread_core), (last + 8, gather_diag),
        None,
        (last + 4, finish), (LAG + 1, leading), (last + 4, settle),
    )

    @pl.loop(0, nodes + last + 8)
    def _(n):
        for entry in stages:
            if entry is None:
                @pl.loop(0, long_hops)
                def _(i):
                    t = long_hops - 1 - i
                    s = n - (LAG + 1) - t

                    @pl.when((s >= 0) & (s < nodes))
                    def _():
                        ring(s, t)
            else:
                lag, work = entry
                s = n - lag

                @pl.when((s >= 0) & (s < nodes))
                def _():
                    work(s)

        @pl.when(n == LAG - 1)
        def _():
            wait_for(af.at[core], a_sem.at[0])
            wait_for(af.at[1 - core], a_sem.at[2])

            @pl.loop(0, slots)
            def _(k):
                for h in range(2):
                    rows, cols = ahi.shape[1], ahi.shape[2] // 2
                    high, low = halves(af[h, k].reshape(rows, cols))
                    ahi[k, :, h * cols:(h + 1) * cols] = high
                    alo[k, :, h * cols:(h + 1) * cols] = low

    wait_for(af.at[core], a_sem.at[1])

    @pl.loop(0, nodes)
    def _(s):
        wait_for(drow.at[s, pl.ds(0, NR - 1)], d_s.at[s, 0])
        wait_for(ez.at[s, pl.ds(0, 2 * NZ - 1)], d_s.at[s, 1])
        wait_for(gr.at[s, core, r, pl.ds(0, 3)], d_s.at[s, 2])
        wait_for(gr.at[s, core, pl.ds(0, NR - 1)], d_s.at[s, 3])
        wait_for(dmate.at[s], d_s.at[s, 4])
        wait_for(gr.at[s, core], d_s.at[s, 5])
        wait_for(off.at[s], o_sem.at[0, s])
        wait_for(diag.at[s], o_sem.at[1, s])


def hand_over(off_ref, diag_ref, off_out, diag_out, off, diag, sems):
    pairs = ((diag_ref, diag, diag_out), (off_ref, off, off_out))
    pieces = diag.shape[0]
    for k in range(pieces):
        for i, (src, held, _) in enumerate(pairs):
            pltpu.make_async_copy(src.at[k], held.at[k], sems.at[0, i, k]).start()
    for k in range(pieces):
        for i, (src, held, dst) in enumerate(pairs):
            pltpu.make_async_copy(src.at[k], held.at[k], sems.at[0, i, k]).wait()
            pltpu.make_async_copy(held.at[k], dst.at[k], sems.at[1, i, k]).start()
    for k in range(pieces):
        for i, (_, held, dst) in enumerate(pairs):
            pltpu.make_async_copy(held.at[k], dst.at[k], sems.at[1, i, k]).wait()


def body(ancestor_inverse, panel, diag_inverse, structure, block_slot):
    nodes, slots, sub, width = panel.shape
    group = 1
    groups = nodes // group
    lane = width // 2
    flat = slots * sub
    blocks = ancestor_inverse.reshape(slots, 2 * NZ, 2, sub, 2 * width)
    rows, depth = width // 2, 4 * width
    smem = pl.BlockSpec(memory_space=pltpu.SMEM)
    hbm = pl.BlockSpec(memory_space=pl.ANY)
    dma = pltpu.SemaphoreType.DMA
    shapes = (
        jax.ShapeDtypeStruct((nodes, slots, sub, width), F32),
        jax.ShapeDtypeStruct((nodes, width, width), F32),
    )
    off, diag = pl.pallas_call(
        functools.partial(kernel, group),
        out_shape=shapes,
        in_specs=[smem, smem, hbm, hbm, hbm],
        out_specs=(hbm, hbm),
        scratch_shapes=[
            pltpu.VMEM((nodes, slots, sub, width), F32),
            pltpu.VMEM((nodes, width, width), F32),
            pltpu.SMEM(block_slot.shape, jnp.int32),
            pltpu.SMEM((nodes, CAP), jnp.int32),
            pltpu.SMEM((nodes, slots), jnp.int32),
            pltpu.SMEM((nodes, slots), jnp.int32),
            pltpu.VMEM((nodes, slots, sub, width), F32),
            pltpu.VMEM((nodes, width, width), F32),
            pltpu.VMEM((2, slots, 2 * NZ, sub, 2 * width), F32),
            pltpu.VMEM((slots, rows, depth), BF16),
            pltpu.VMEM((slots, rows, depth), BF16),
            pltpu.VMEM((nodes, 2, NR, sub, lane), F32),
            pltpu.VMEM((nodes, 2, flat, width), F32),
            pltpu.VMEM((groups, NR, group, 2, sub, lane), F32),
            pltpu.VMEM((nodes, NR, 2 * NZ, 2, sub, lane), F32),
            pltpu.VMEM((depth, width), BF16),
            pltpu.VMEM((depth, width), BF16),
            pltpu.VMEM((nodes, NZ, CAP, 2, sub, width), F32),
            pltpu.VMEM((nodes, NZ - 1, CAP, 2, sub, width), F32),
            pltpu.VMEM((nodes, CAP, sub, width), F32),
            pltpu.VMEM((CAP, sub, width), F32),
            pltpu.VMEM((2 * flat, width), F32),
            pltpu.VMEM((nodes, 2, NR, 4, sub, lane), F32),
            pltpu.VMEM((nodes, NR, 4, sub, lane), F32),
            pltpu.VMEM((nodes, NR, 4, sub, lane), F32),
            pltpu.VMEM((nodes, NR, 4, sub, lane), F32),
            pltpu.VMEM((nodes, 4, sub, lane), F32),
            pltpu.VMEM((nodes, 2 * NZ, sub, lane), F32),
            pltpu.VMEM((nodes, 2, NR, 4, sub, lane), F32),
            pltpu.VMEM((nodes, width, width), F32),
            dma((2,)), dma((2, nodes)), dma((3,)),
            dma((groups,)), dma((groups,)), dma((groups,)),
            dma((groups,)), dma((groups,)), dma((groups,)),
            dma((nodes,)), dma((nodes,)),
            dma((nodes, 2)), dma((nodes, 2)),
            dma((nodes, 2)), dma((nodes, 2)),
            dma((nodes,)), dma((nodes,)),
            dma((nodes,)), dma((nodes,)),
            dma((nodes, NZ - 1)), dma((nodes, NZ - 1)),
            dma((nodes,)), dma((nodes,)),
            dma((nodes, 6)), dma((nodes, 6)),
        ],
        compiler_params=pltpu.CompilerParams(
            collective_id=0, has_side_effects=True, vmem_limit_bytes=62 * 1024 * 1024
        ),
        name="invert_level",
    )(structure, block_slot, blocks, panel, diag_inverse)
    return pl.pallas_call(
        hand_over,
        out_shape=shapes,
        in_specs=[hbm, hbm],
        out_specs=(hbm, hbm),
        scratch_shapes=[
            pltpu.VMEM(off.shape, F32), pltpu.VMEM(diag.shape, F32), dma((2, 2, nodes)),
        ],
        name="hand_over",
    )(off, diag)


def solution(mesh):
    in_specs = (P("row", "col"), P(None, "row", "col", None), P(), P(), P())
    out_specs = (P(None, "row", "col", None), P())
    return jax.shard_map(body, mesh=mesh, in_specs=in_specs, out_specs=out_specs, check_vma=False)
```

```python
import functools

import jax
import jax.numpy as jnp
from jax import lax
from jax.experimental import pallas as pl
from jax.experimental.pallas import tpu as pltpu
from jax.sharding import PartitionSpec as P

F32 = jnp.float32
BF16 = jnp.bfloat16
MESH = pl.DeviceIdType.MESH
HIGHEST = lax.Precision.HIGHEST

NR = 8
NZ = 8
CAP = 6
LAG = 3


def halves(value):
    high = value.astype(BF16)
    return high, (value - high.astype(F32)).astype(BF16)


def wait_for(ref, sem):
    pltpu.make_async_copy(ref, ref, sem).wait()


def kernel(
    group,
    structure, place, a_ref, panel_ref, dinv_ref, off_ref, diag_ref,
    off, diag, bits, ids, pos, mask, panel, dinv,
    af, ahi, alo, nsrc, nboth, abuf, nbuf, nhi, nlo, ybuf, rbuf, pbuf, yfin, fexp,
    dbuf, dmate, dsum, drow, ebuf, ez, gr, lead,
    in_sem, o_sem, a_sem, s1_s, s1_r, s1_l, s2_s, s2_r, s2_l,
    c1_s, c1_r, c2_s, c2_r, c3_s, c3_r, sh_s, sh_r, n_s, n_r,
    ring_s, ring_r, p_s, p_r, d_s, d_r,
):
    nodes, slots, sub, width = panel.shape
    lane = width // 2
    flat = slots * sub
    groups = nodes // group
    r = lax.axis_index("row")
    c = lax.axis_index("col")
    z = c // 4
    yh = lax.rem(c // 2, 2)
    core = lax.rem(c, 2)
    zy = c // 2
    x = r // 2
    yl = lax.rem(r, 2)

    def send(src, dst, ssem, rsem, where):
        pltpu.make_async_remote_copy(
            src_ref=src, dst_ref=dst, send_sem=ssem, recv_sem=rsem,
            device_id=where, device_id_type=MESH,
        ).start()

    def at_row(t):
        return {"row": t, "col": c}

    def at_zy(t):
        return {"row": r, "col": t * 2 + core}

    plane = r * 2 + yh

    def at_plane(t):
        return {"row": t // 2, "col": (z * 2 + lax.rem(t, 2)) * 2 + core}

    def plane_peer(i):
        return lax.rem(plane + i, 2 * NR)

    def row_peer(i):
        return lax.rem(r + i, NR)

    def zy_peer(i):
        return lax.rem(zy + i, 2 * NZ)

    mate = {"row": r, "col": zy * 2 + 1 - core}
    across = at_zy(z * 2 + 1 - yh)

    load_panel = pltpu.make_async_copy(panel_ref, panel, in_sem.at[0])
    load_dinv = pltpu.make_async_copy(dinv_ref, dinv, in_sem.at[1])
    own_a = pltpu.make_async_copy(a_ref.at[:, :, core], af.at[core], a_sem.at[0])
    load_panel.start()
    load_dinv.start()
    own_a.start()

    barrier = pltpu.get_barrier_semaphore()

    def greet(where):
        pl.semaphore_signal(barrier, inc=1, device_id=where, device_id_type=MESH)

    @pl.loop(1, 2 * NZ)
    def _(i):
        greet(at_zy(zy_peer(i)))

    @pl.loop(1, NR)
    def _(i):
        greet(at_row(row_peer(i)))
        greet(at_plane(row_peer(i) * 2 + 1 - yh))

    greet(mate)

    @pl.loop(0, place.shape[0])
    def _(b):
        slot = place[b] - r * slots
        bits[b] = sum((slot == i).astype(jnp.int32) * (1 << i) for i in range(slots))

    @pl.loop(0, nodes)
    def _(s):
        used = bits[structure[s, 0]]
        for k in range(1, structure.shape[1]):
            used = used + bits[structure[s, k]]
        seen = [lax.shift_right_logical(used, jnp.int32(i)) & 1 for i in range(slots)]
        for i in range(slots):
            mask[s, i] = seen[i]

    load_panel.wait()
    load_dinv.wait()

    @pl.loop(0, nodes)
    def _(s):
        value = jnp.dot(
            panel[s].reshape(flat, width), dinv[s],
            precision=HIGHEST, preferred_element_type=F32,
        )
        for k in range(slots):
            part = value[k * sub:(k + 1) * sub] * mask[s, k].astype(F32)
            nboth[s, 0, k * sub:(k + 1) * sub, :] = part
            for h in range(2):
                nsrc[s, k // 4, (k % 4) * 2 + h] = part[:, h * lane:(h + 1) * lane]

    pl.semaphore_wait(barrier, 2 * NZ - 1 + 2 * NR - 1)

    def exchange_row(g):
        span = pl.ds(g * group, group)
        pltpu.make_async_copy(nsrc.at[span, :, r], abuf.at[g, r], s1_l.at[g]).start()

        @pl.loop(1, NR)
        def _(i):
            p = lax.rem(r + i, NR)
            send(nsrc.at[span, :, p], abuf.at[g, r], s1_s.at[g], s1_r.at[g], {"row": p, "col": c})

    def exchange_col(g):
        span = pl.ds(g * group, group)
        wait_for(abuf.at[g, r], s1_l.at[g])
        wait_for(abuf.at[g, pl.ds(0, NR - 1)], s1_r.at[g])
        pltpu.make_async_copy(abuf.at[g, z, :, yh], nbuf.at[span, r, zy, core], s2_l.at[g]).start()

        @pl.loop(1, 2 * NZ)
        def _(i):
            t = zy_peer(i)
            send(
                abuf.at[g, t // 2, :, lax.rem(t, 2)], nbuf.at[span, r, zy, core],
                s2_s.at[g], s2_r.at[g], at_zy(t),
            )

    exchange_row(0)
    exchange_row(1)
    send(a_ref.at[:, :, 1 - core], af.at[core], a_sem.at[1], a_sem.at[2], mate)
    exchange_col(0)

    @pl.loop(0, nodes)
    def _(s):
        before = jnp.int32(0)
        spots = []
        for i in range(slots):
            pos[s, i] = before * mask[s, i]
            spots.append(before)
            before = before + mask[s, i]
        for k in range(CAP):
            found = jnp.int32(0)
            for i in range(slots):
                found = found + i * mask[s, i] * (spots[i] == k).astype(jnp.int32)
            ids[s, k] = found

    @pl.loop(2, groups)
    def _(g):
        exchange_row(g)

    exchange_col(1)

    right = {"row": lax.rem(x + 1, 4) * 2 + yl, "col": c}
    left = {"row": lax.rem(x + 3, 4) * 2 + yl, "col": c}
    other = x * 2 + 1 - yl
    twin = {"row": other, "col": c}
    xl, xr, xo = lax.rem(x + 3, 4), lax.rem(x + 1, 4), lax.rem(x + 2, 4)
    way = 1 - 2 * core
    long_hops, short_hops = NZ // 2, NZ // 2 - 1

    def z_at(d):
        return lax.rem(z + d + NZ, NZ)

    after_long = at_zy(z_at(-way) * 2 + yh)
    after_short = at_zy(z_at(way) * 2 + yh)

    def pass_long(s, t):
        part = ybuf.at[s, z_at(-way * (long_hops - t))]
        send(part, rbuf.at[s, t], ring_s.at[s, t], ring_r.at[s, t], after_long)

    def pass_short(s, t):
        part = ybuf.at[s, z_at(way * (short_hops - t))]
        k = long_hops + t
        send(part, rbuf.at[s, k], ring_s.at[s, k], ring_r.at[s, k], after_short)

    def block(s, p):
        return nbuf.at[s, p, :, core]

    def two(s, p):
        return nbuf.at[s, pl.ds(p, 2), :, core]

    def share(s, part):
        send(part, part, sh_s.at[s], sh_r.at[s], mate)

    def relay_one(s):
        wait_for(nbuf.at[pl.ds(0, group), r, zy, core], s2_l.at[s])
        wait_for(nbuf.at[pl.ds(0, group), r, pl.ds(0, 2 * NZ - 1), core], s2_r.at[s])

        @pl.when(s + 2 < groups)
        def _():
            exchange_col(s + 2)

        mine = block(s, r)
        send(mine, mine, c1_s.at[s], c1_r.at[s], twin)
        send(mine, mine, c2_s.at[s, 0], c2_r.at[s, 0], right)
        send(mine, mine, c2_s.at[s, 1], c2_r.at[s, 1], left)
        share(s, mine)

    def relay_two(s):
        wait_for(block(s, r), c1_r.at[s])
        theirs = block(s, other)
        send(theirs, theirs, c2_s.at[s, 0], c2_r.at[s, 0], right)
        send(theirs, theirs, c2_s.at[s, 1], c2_r.at[s, 1], left)
        share(s, theirs)

    def relay_three(s):
        wait_for(two(s, 0), c2_r.at[s, 0])
        send(block(s, 2 * xl), block(s, 2 * xl), c3_s.at[s, 0], c3_r.at[s, 0], right)
        share(s, two(s, 2 * xl))
        wait_for(two(s, 0), c2_r.at[s, 1])
        send(block(s, 2 * xr + 1), block(s, 2 * xr + 1), c3_s.at[s, 1], c3_r.at[s, 1], left)
        share(s, two(s, 2 * xr))

    def relay_four(s):
        wait_for(block(s, r), c3_r.at[s, 0])
        wait_for(block(s, r), c3_r.at[s, 1])
        share(s, two(s, 2 * xo))

    def multiply(s):
        wait_for(nbuf.at[s, :, :, 1 - core], sh_r.at[s])
        for j in range(4):
            for h in range(2):
                high, low = halves(nbuf[s, 2 * j + h].reshape(width, lane))
                nhi[j * width:(j + 1) * width, h * lane:(h + 1) * lane] = high
                nlo[j * width:(j + 1) * width, h * lane:(h + 1) * lane] = low

        @pl.loop(0, CAP // 2)
        def _(m):
            one, two = ids[s, 2 * m], ids[s, 2 * m + 1]
            high = jnp.concatenate([ahi[one], ahi[two]], axis=0)
            low = jnp.concatenate([alo[one], alo[two]], axis=0)
            total = jnp.dot(high, nhi[...], preferred_element_type=F32)
            total += jnp.dot(high, nlo[...], preferred_element_type=F32)
            total += jnp.dot(low, nhi[...], preferred_element_type=F32)
            rows = ahi.shape[1]
            ybuf[s, :, 2 * m] = total[:rows].reshape(NZ, 2, sub, width)
            ybuf[s, :, 2 * m + 1] = total[rows:].reshape(NZ, 2, sub, width)
        pass_long(s, 0)
        pass_short(s, 0)
        send(nboth.at[s, 0], nboth.at[s, 1], n_s.at[s], n_r.at[s], across)

    def ring(s, t):
        wait_for(rbuf.at[s, t], ring_r.at[s, t])
        b = z_at(-way * (long_hops - 1 - t))
        ybuf[s, b] = ybuf[s, b] + rbuf[s, t]

        @pl.when(t < long_hops - 1)
        def _():
            pass_long(s, t + 1)
            k = long_hops + t
            wait_for(rbuf.at[s, k], ring_r.at[s, k])
            f = z_at(way * (short_hops - 1 - t))
            ybuf[s, f] = ybuf[s, f] + rbuf[s, k]

            @pl.when(t < short_hops - 1)
            def _():
                pass_short(s, t + 1)

        @pl.when(t == long_hops - 1)
        def _():
            send(ybuf.at[s, z, :, 1 - yh], pbuf.at[s], p_s.at[s], p_r.at[s], across)
            wait_for(nboth.at[s, 1], n_r.at[s])
            for k in range(slots):
                scale = mask[s, k].astype(F32)
                fexp[k * sub:(k + 1) * sub, :] = ybuf[s, z, pos[s, k], yh] * scale
                fexp[flat + k * sub:flat + (k + 1) * sub, :] = ybuf[s, z, pos[s, k], 1 - yh] * scale
            part = lax.dot_general(
                nboth[s].reshape(2 * flat, width), fexp[...], (((0,), (0,)), ((), ())),
                precision=HIGHEST, preferred_element_type=F32,
            )
            for h in range(2):
                dbuf[s, h] = part[:, h * lane:(h + 1) * lane].reshape(NR, 4, sub, lane)
            send(dbuf.at[s, 1 - core], dmate.at[s], d_s.at[s, 4], d_r.at[s, 4], mate)

    def diag_row(s):
        wait_for(dmate.at[s], d_r.at[s, 4])
        dsum[s] = dbuf[s, core] + dmate[s]
        drow[s, plane] = dsum[s, r, pl.ds(2 * yh, 2)]

        @pl.loop(1, 2 * NR)
        def _(i):
            p = plane_peer(i)
            mine = dsum.at[s, p // 2, pl.ds(2 * lax.rem(p, 2), 2)]
            send(mine, drow.at[s, plane], d_s.at[s, 0], d_r.at[s, 0], at_plane(p))

    def finish(s):
        wait_for(pbuf.at[s], p_r.at[s])
        yfin[...] = ybuf[s, z, :, yh] + pbuf[s]
        for k in range(slots):
            off[s, k] = yfin[pos[s, k]] * (-mask[s, k].astype(F32))
        pltpu.make_async_copy(off.at[s], off_ref.at[s], o_sem.at[0, s]).start()

    def diag_z(s):
        wait_for(drow.at[s, pl.ds(0, 2 * NR - 1)], d_r.at[s, 0])
        ebuf[s] = jnp.sum(drow[s], axis=0)
        ez[s, z] = ebuf[s, lax.rem(z, 2)]

        @pl.loop(1, NZ)
        def _(i):
            t = lax.rem(z + i, NZ)
            send(ebuf.at[s, lax.rem(t, 2)], ez.at[s, z], d_s.at[s, 1], d_r.at[s, 1], at_zy(t * 2 + yh))

    tile = r * 4 + yh * 2

    def spread_z(s):
        wait_for(ez.at[s, pl.ds(0, NZ - 1)], d_r.at[s, 1])
        u = tile + lax.rem(z, 2)
        here = gr.at[s, core, u]
        gr[s, core, u] = jnp.sum(ez[s], axis=0)
        send(here, here, d_s.at[s, 2], d_r.at[s, 2], at_zy((z + 1 - 2 * lax.rem(z, 2)) * 2 + yh))

    def spread_row(s):
        wait_for(gr.at[s, core, tile], d_r.at[s, 2])
        here = gr.at[s, core, pl.ds(tile, 2)]

        @pl.loop(1, 2 * NR)
        def _(i):
            send(here, here, d_s.at[s, 3], d_r.at[s, 3], at_plane(plane_peer(i)))

    def spread_core(s):
        wait_for(gr.at[s, core, pl.ds(0, 4 * NR - 2)], d_r.at[s, 3])
        here = gr.at[s, core]
        send(here, here, d_s.at[s, 5], d_r.at[s, 5], mate)

    def gather_diag(s):
        wait_for(gr.at[s, 1 - core], d_r.at[s, 5])
        for h in range(2):
            here = slice(h * lane, (h + 1) * lane)
            diag[s, :, here] = lead[s, :, here] + gr[s, h].reshape(width, lane)
        pltpu.make_async_copy(diag.at[s], diag_ref.at[s], o_sem.at[1, s]).start()

    def leading(s):
        lead[s] = lax.dot_general(
            dinv[s], dinv[s], (((0,), (0,)), ((), ())),
            precision=HIGHEST, preferred_element_type=F32,
        )

    def settle(s):
        wait_for(abuf.at[s, pl.ds(0, NR - 1)], s1_s.at[s])
        wait_for(nbuf.at[pl.ds(0, group), r, pl.ds(0, 2 * NZ - 1), core], s2_s.at[s])
        wait_for(block(s, r), c1_s.at[s])
        for w in range(2):
            wait_for(two(s, 0), c2_s.at[s, w])
            wait_for(block(s, r), c3_s.at[s, w])
        wait_for(nbuf.at[s, :, :, core], sh_s.at[s])
        wait_for(nboth.at[s, 0], n_s.at[s])
        for t in range(NZ - 1):
            wait_for(rbuf.at[s, t], ring_s.at[s, t])
        wait_for(pbuf.at[s], p_s.at[s])

    last = LAG + long_hops
    stages = (
        (2, relay_three), (1, relay_two), (0, relay_one), (3, relay_four), (LAG, multiply),
        (last + 1, diag_row), (last + 2, diag_z), (last + 4, spread_z), (last + 5, spread_row),
        (last + 7, spread_core), (last + 8, gather_diag),
        None,
        (last + 4, finish), (LAG + 1, leading), (last + 4, settle),
    )

    @pl.loop(0, nodes + last + 8)
    def _(n):
        for entry in stages:
            if entry is None:
                @pl.loop(0, long_hops)
                def _(i):
                    t = long_hops - 1 - i
                    s = n - (LAG + 1) - t

                    @pl.when((s >= 0) & (s < nodes))
                    def _():
                        ring(s, t)
            else:
                lag, work = entry
                s = n - lag

                @pl.when((s >= 0) & (s < nodes))
                def _():
                    work(s)

        @pl.when(n == LAG - 1)
        def _():
            wait_for(af.at[core], a_sem.at[0])
            wait_for(af.at[1 - core], a_sem.at[2])

            @pl.loop(0, slots)
            def _(k):
                for h in range(2):
                    rows, cols = ahi.shape[1], ahi.shape[2] // 2
                    high, low = halves(af[h, k].reshape(rows, cols))
                    ahi[k, :, h * cols:(h + 1) * cols] = high
                    alo[k, :, h * cols:(h + 1) * cols] = low

    wait_for(af.at[core], a_sem.at[1])

    @pl.loop(0, nodes)
    def _(s):
        wait_for(drow.at[s, pl.ds(0, 2 * NR - 1)], d_s.at[s, 0])
        wait_for(ez.at[s, pl.ds(0, NZ - 1)], d_s.at[s, 1])
        wait_for(gr.at[s, core, tile], d_s.at[s, 2])
        wait_for(gr.at[s, core, pl.ds(0, 4 * NR - 2)], d_s.at[s, 3])
        wait_for(dmate.at[s], d_s.at[s, 4])
        wait_for(gr.at[s, core], d_s.at[s, 5])
        wait_for(off.at[s], o_sem.at[0, s])
        wait_for(diag.at[s], o_sem.at[1, s])


def hand_over(off_ref, diag_ref, off_out, diag_out, off, diag, sems):
    pairs = ((diag_ref, diag, diag_out), (off_ref, off, off_out))
    pieces = diag.shape[0]
    for k in range(pieces):
        for i, (src, held, _) in enumerate(pairs):
            pltpu.make_async_copy(src.at[k], held.at[k], sems.at[0, i, k]).start()
    for k in range(pieces):
        for i, (src, held, dst) in enumerate(pairs):
            pltpu.make_async_copy(src.at[k], held.at[k], sems.at[0, i, k]).wait()
            pltpu.make_async_copy(held.at[k], dst.at[k], sems.at[1, i, k]).start()
    for k in range(pieces):
        for i, (_, held, dst) in enumerate(pairs):
            pltpu.make_async_copy(held.at[k], dst.at[k], sems.at[1, i, k]).wait()


def body(ancestor_inverse, panel, diag_inverse, structure, block_slot):
    nodes, slots, sub, width = panel.shape
    group = 1
    groups = nodes // group
    lane = width // 2
    flat = slots * sub
    blocks = ancestor_inverse.reshape(slots, 2 * NZ, 2, sub, 2 * width)
    rows, depth = width // 2, 4 * width
    smem = pl.BlockSpec(memory_space=pltpu.SMEM)
    hbm = pl.BlockSpec(memory_space=pl.ANY)
    dma = pltpu.SemaphoreType.DMA
    shapes = (
        jax.ShapeDtypeStruct((nodes, slots, sub, width), F32),
        jax.ShapeDtypeStruct((nodes, width, width), F32),
    )
    off, diag = pl.pallas_call(
        functools.partial(kernel, group),
        out_shape=shapes,
        in_specs=[smem, smem, hbm, hbm, hbm],
        out_specs=(hbm, hbm),
        scratch_shapes=[
            pltpu.VMEM((nodes, slots, sub, width), F32),
            pltpu.VMEM((nodes, width, width), F32),
            pltpu.SMEM(block_slot.shape, jnp.int32),
            pltpu.SMEM((nodes, CAP), jnp.int32),
            pltpu.SMEM((nodes, slots), jnp.int32),
            pltpu.SMEM((nodes, slots), jnp.int32),
            pltpu.VMEM((nodes, slots, sub, width), F32),
            pltpu.VMEM((nodes, width, width), F32),
            pltpu.VMEM((2, slots, 2 * NZ, sub, 2 * width), F32),
            pltpu.VMEM((slots, rows, depth), BF16),
            pltpu.VMEM((slots, rows, depth), BF16),
            pltpu.VMEM((nodes, 2, NR, sub, lane), F32),
            pltpu.VMEM((nodes, 2, flat, width), F32),
            pltpu.VMEM((groups, NR, group, 2, sub, lane), F32),
            pltpu.VMEM((nodes, NR, 2 * NZ, 2, sub, lane), F32),
            pltpu.VMEM((depth, width), BF16),
            pltpu.VMEM((depth, width), BF16),
            pltpu.VMEM((nodes, NZ, CAP, 2, sub, width), F32),
            pltpu.VMEM((nodes, NZ - 1, CAP, 2, sub, width), F32),
            pltpu.VMEM((nodes, CAP, sub, width), F32),
            pltpu.VMEM((CAP, sub, width), F32),
            pltpu.VMEM((2 * flat, width), F32),
            pltpu.VMEM((nodes, 2, NR, 4, sub, lane), F32),
            pltpu.VMEM((nodes, NR, 4, sub, lane), F32),
            pltpu.VMEM((nodes, NR, 4, sub, lane), F32),
            pltpu.VMEM((nodes, 2 * NR, 2, sub, lane), F32),
            pltpu.VMEM((nodes, 2, sub, lane), F32),
            pltpu.VMEM((nodes, NZ, sub, lane), F32),
            pltpu.VMEM((nodes, 2, 4 * NR, sub, lane), F32),
            pltpu.VMEM((nodes, width, width), F32),
            dma((2,)), dma((2, nodes)), dma((3,)),
            dma((groups,)), dma((groups,)), dma((groups,)),
            dma((groups,)), dma((groups,)), dma((groups,)),
            dma((nodes,)), dma((nodes,)),
            dma((nodes, 2)), dma((nodes, 2)),
            dma((nodes, 2)), dma((nodes, 2)),
            dma((nodes,)), dma((nodes,)),
            dma((nodes,)), dma((nodes,)),
            dma((nodes, NZ - 1)), dma((nodes, NZ - 1)),
            dma((nodes,)), dma((nodes,)),
            dma((nodes, 6)), dma((nodes, 6)),
        ],
        compiler_params=pltpu.CompilerParams(
            collective_id=0, has_side_effects=True, vmem_limit_bytes=62 * 1024 * 1024
        ),
        name="invert_level",
    )(structure, block_slot, blocks, panel, diag_inverse)
    return pl.pallas_call(
        hand_over,
        out_shape=shapes,
        in_specs=[hbm, hbm],
        out_specs=(hbm, hbm),
        scratch_shapes=[
            pltpu.VMEM(off.shape, F32), pltpu.VMEM(diag.shape, F32), dma((2, 2, nodes)),
        ],
        name="hand_over",
    )(off, diag)


def solution(mesh):
    in_specs = (P("row", "col"), P(None, "row", "col", None), P(), P(), P())
    out_specs = (P(None, "row", "col", None), P())
    return jax.shard_map(body, mesh=mesh, in_specs=in_specs, out_specs=out_specs, check_vma=False)
```

```python
import functools

import jax
import jax.numpy as jnp
from jax import lax
from jax.experimental import pallas as pl
from jax.experimental.pallas import tpu as pltpu
from jax.sharding import PartitionSpec as P

F32 = jnp.float32
BF16 = jnp.bfloat16
MESH = pl.DeviceIdType.MESH
HIGHEST = lax.Precision.HIGHEST

NR = 8
NZ = 8
CAP = 6
LAG = 3


def halves(value):
    high = value.astype(BF16)
    return high, (value - high.astype(F32)).astype(BF16)


def wait_for(ref, sem):
    pltpu.make_async_copy(ref, ref, sem).wait()


def kernel(
    group,
    structure, place, a_ref, panel_ref, dinv_ref, off, diag,
    bits, ids, pos, mask, panel, dinv,
    af, ahi, alo, nsrc, nboth, abuf, nbuf, nhi, nlo, ybuf, rbuf, pbuf, yfin, fexp,
    dbuf, dmate, dsum, drow, ebuf, ez, gr, lead,
    in_sem, a_sem, s1_s, s1_r, s1_l, s2_s, s2_r, s2_l,
    c1_s, c1_r, c2_s, c2_r, c3_s, c3_r, sh_s, sh_r, n_s, n_r,
    ring_s, ring_r, p_s, p_r, d_s, d_r,
):
    nodes, slots, sub, width = panel.shape
    lane = width // 2
    flat = slots * sub
    groups = nodes // group
    r = lax.axis_index("row")
    c = lax.axis_index("col")
    z = c // 4
    yh = lax.rem(c // 2, 2)
    core = lax.rem(c, 2)
    zy = c // 2
    x = r // 2
    yl = lax.rem(r, 2)

    def send(src, dst, ssem, rsem, where):
        pltpu.make_async_remote_copy(
            src_ref=src, dst_ref=dst, send_sem=ssem, recv_sem=rsem,
            device_id=where, device_id_type=MESH,
        ).start()

    def at_row(t):
        return {"row": t, "col": c}

    def at_zy(t):
        return {"row": r, "col": t * 2 + core}

    plane = r * 2 + yh

    def at_plane(t):
        return {"row": t // 2, "col": (z * 2 + lax.rem(t, 2)) * 2 + core}

    def plane_peer(i):
        return lax.rem(plane + i, 2 * NR)

    def row_peer(i):
        return lax.rem(r + i, NR)

    def zy_peer(i):
        return lax.rem(zy + i, 2 * NZ)

    mate = {"row": r, "col": zy * 2 + 1 - core}
    across = at_zy(z * 2 + 1 - yh)

    load_panel = pltpu.make_async_copy(panel_ref, panel, in_sem.at[0])
    load_dinv = pltpu.make_async_copy(dinv_ref, dinv, in_sem.at[1])
    own_a = pltpu.make_async_copy(a_ref.at[:, :, core], af.at[core], a_sem.at[0])
    load_panel.start()
    load_dinv.start()
    own_a.start()

    barrier = pltpu.get_barrier_semaphore()

    def greet(where):
        pl.semaphore_signal(barrier, inc=1, device_id=where, device_id_type=MESH)

    @pl.loop(1, 2 * NZ)
    def _(i):
        greet(at_zy(zy_peer(i)))

    @pl.loop(1, NR)
    def _(i):
        greet(at_row(row_peer(i)))
        greet(at_plane(row_peer(i) * 2 + 1 - yh))

    greet(mate)

    for i in range(bits.shape[0]):
        bits[i] = jnp.int32(0)
    for i in range(slots):
        bits[r * slots + i] = jnp.int32(1 << i)

    def mark(s):
        used = bits[place[structure[s, 0]]]
        for k in range(1, structure.shape[1]):
            used = used + bits[place[structure[s, k]]]
        for i in range(slots):
            mask[s, i] = lax.shift_right_logical(used, jnp.int32(i)) & 1

    def normalize(s):
        value = jnp.dot(
            panel[s].reshape(flat, width), dinv[s],
            precision=HIGHEST, preferred_element_type=F32,
        )
        for k in range(slots):
            part = value[k * sub:(k + 1) * sub] * mask[s, k].astype(F32)
            nboth[s, 0, k * sub:(k + 1) * sub, :] = part
            for h in range(2):
                nsrc[s, k // 4, (k % 4) * 2 + h] = part[:, h * lane:(h + 1) * lane]

    mark(0)
    load_panel.wait()
    load_dinv.wait()
    normalize(0)
    pl.semaphore_wait(barrier, 2 * NZ - 1 + 2 * NR - 1)

    def exchange_row(g):
        span = pl.ds(g * group, group)
        pltpu.make_async_copy(nsrc.at[span, :, r], abuf.at[g, r], s1_l.at[g]).start()

        @pl.loop(1, NR)
        def _(i):
            p = lax.rem(r + i, NR)
            send(nsrc.at[span, :, p], abuf.at[g, r], s1_s.at[g], s1_r.at[g], {"row": p, "col": c})

    def exchange_col(g):
        span = pl.ds(g * group, group)
        wait_for(abuf.at[g, r], s1_l.at[g])
        wait_for(abuf.at[g, pl.ds(0, NR - 1)], s1_r.at[g])
        pltpu.make_async_copy(abuf.at[g, z, :, yh], nbuf.at[span, r, zy, core], s2_l.at[g]).start()

        @pl.loop(1, 2 * NZ)
        def _(i):
            t = zy_peer(i)
            send(
                abuf.at[g, t // 2, :, lax.rem(t, 2)], nbuf.at[span, r, zy, core],
                s2_s.at[g], s2_r.at[g], at_zy(t),
            )

    exchange_row(0)
    mark(1)
    normalize(1)
    exchange_row(1)
    send(a_ref.at[:, :, 1 - core], af.at[core], a_sem.at[1], a_sem.at[2], mate)

    @pl.loop(2, nodes)
    def _(s):
        mark(s)
        normalize(s)

    exchange_col(0)

    @pl.loop(0, nodes)
    def _(s):
        before = jnp.int32(0)
        spots = []
        for i in range(slots):
            pos[s, i] = before * mask[s, i]
            spots.append(before)
            before = before + mask[s, i]
        for k in range(CAP):
            found = jnp.int32(0)
            for i in range(slots):
                found = found + i * mask[s, i] * (spots[i] == k).astype(jnp.int32)
            ids[s, k] = found

    @pl.loop(2, groups)
    def _(g):
        exchange_row(g)

    exchange_col(1)

    right = {"row": lax.rem(x + 1, 4) * 2 + yl, "col": c}
    left = {"row": lax.rem(x + 3, 4) * 2 + yl, "col": c}
    other = x * 2 + 1 - yl
    twin = {"row": other, "col": c}
    xl, xr, xo = lax.rem(x + 3, 4), lax.rem(x + 1, 4), lax.rem(x + 2, 4)
    way = 1 - 2 * core
    long_hops, short_hops = NZ // 2, NZ // 2 - 1

    def z_at(d):
        return lax.rem(z + d + NZ, NZ)

    after_long = at_zy(z_at(-way) * 2 + yh)
    after_short = at_zy(z_at(way) * 2 + yh)

    def pass_long(s, t):
        part = ybuf.at[s, z_at(-way * (long_hops - t))]
        send(part, rbuf.at[s, t], ring_s.at[s, t], ring_r.at[s, t], after_long)

    def pass_short(s, t):
        part = ybuf.at[s, z_at(way * (short_hops - t))]
        k = long_hops + t
        send(part, rbuf.at[s, k], ring_s.at[s, k], ring_r.at[s, k], after_short)

    def block(s, p):
        return nbuf.at[s, p, :, core]

    def two(s, p):
        return nbuf.at[s, pl.ds(p, 2), :, core]

    def share(s, part):
        send(part, part, sh_s.at[s], sh_r.at[s], mate)

    def relay_one(s):
        wait_for(nbuf.at[pl.ds(0, group), r, zy, core], s2_l.at[s])
        wait_for(nbuf.at[pl.ds(0, group), r, pl.ds(0, 2 * NZ - 1), core], s2_r.at[s])

        @pl.when(s + 2 < groups)
        def _():
            exchange_col(s + 2)

        mine = block(s, r)
        send(mine, mine, c1_s.at[s], c1_r.at[s], twin)
        send(mine, mine, c2_s.at[s, 0], c2_r.at[s, 0], right)
        send(mine, mine, c2_s.at[s, 1], c2_r.at[s, 1], left)
        share(s, mine)

    def relay_two(s):
        wait_for(block(s, r), c1_r.at[s])
        theirs = block(s, other)
        send(theirs, theirs, c2_s.at[s, 0], c2_r.at[s, 0], right)
        send(theirs, theirs, c2_s.at[s, 1], c2_r.at[s, 1], left)
        share(s, theirs)

    def relay_three(s):
        wait_for(two(s, 0), c2_r.at[s, 0])
        send(block(s, 2 * xl), block(s, 2 * xl), c3_s.at[s, 0], c3_r.at[s, 0], right)
        share(s, two(s, 2 * xl))
        wait_for(two(s, 0), c2_r.at[s, 1])
        send(block(s, 2 * xr + 1), block(s, 2 * xr + 1), c3_s.at[s, 1], c3_r.at[s, 1], left)
        share(s, two(s, 2 * xr))

    def relay_four(s):
        wait_for(block(s, r), c3_r.at[s, 0])
        wait_for(block(s, r), c3_r.at[s, 1])
        share(s, two(s, 2 * xo))

    def multiply(s):
        wait_for(nbuf.at[s, :, :, 1 - core], sh_r.at[s])
        for j in range(4):
            for h in range(2):
                high, low = halves(nbuf[s, 2 * j + h].reshape(width, lane))
                nhi[j * width:(j + 1) * width, h * lane:(h + 1) * lane] = high
                nlo[j * width:(j + 1) * width, h * lane:(h + 1) * lane] = low

        @pl.loop(0, CAP // 2)
        def _(m):
            one, two = ids[s, 2 * m], ids[s, 2 * m + 1]
            high = jnp.concatenate([ahi[one], ahi[two]], axis=0)
            low = jnp.concatenate([alo[one], alo[two]], axis=0)
            total = jnp.dot(high, nhi[...], preferred_element_type=F32)
            total += jnp.dot(high, nlo[...], preferred_element_type=F32)
            total += jnp.dot(low, nhi[...], preferred_element_type=F32)
            rows = ahi.shape[1]
            ybuf[s, :, 2 * m] = total[:rows].reshape(NZ, 2, sub, width)
            ybuf[s, :, 2 * m + 1] = total[rows:].reshape(NZ, 2, sub, width)
        pass_long(s, 0)
        pass_short(s, 0)
        send(nboth.at[s, 0], nboth.at[s, 1], n_s.at[s], n_r.at[s], across)

    def ring(s, t):
        wait_for(rbuf.at[s, t], ring_r.at[s, t])
        b = z_at(-way * (long_hops - 1 - t))
        ybuf[s, b] = ybuf[s, b] + rbuf[s, t]

        @pl.when(t < long_hops - 1)
        def _():
            pass_long(s, t + 1)
            k = long_hops + t
            wait_for(rbuf.at[s, k], ring_r.at[s, k])
            f = z_at(way * (short_hops - 1 - t))
            ybuf[s, f] = ybuf[s, f] + rbuf[s, k]

            @pl.when(t < short_hops - 1)
            def _():
                pass_short(s, t + 1)

        @pl.when(t == long_hops - 1)
        def _():
            send(ybuf.at[s, z, :, 1 - yh], pbuf.at[s], p_s.at[s], p_r.at[s], across)
            wait_for(nboth.at[s, 1], n_r.at[s])
            for k in range(slots):
                scale = mask[s, k].astype(F32)
                fexp[k * sub:(k + 1) * sub, :] = ybuf[s, z, pos[s, k], yh] * scale
                fexp[flat + k * sub:flat + (k + 1) * sub, :] = ybuf[s, z, pos[s, k], 1 - yh] * scale
            part = lax.dot_general(
                nboth[s].reshape(2 * flat, width), fexp[...], (((0,), (0,)), ((), ())),
                precision=HIGHEST, preferred_element_type=F32,
            )
            for h in range(2):
                dbuf[s, h] = part[:, h * lane:(h + 1) * lane].reshape(NR, 4, sub, lane)
            send(dbuf.at[s, 1 - core], dmate.at[s], d_s.at[s, 4], d_r.at[s, 4], mate)

    def diag_row(s):
        wait_for(dmate.at[s], d_r.at[s, 4])
        dsum[s] = dbuf[s, core] + dmate[s]
        drow[s, plane] = dsum[s, r, pl.ds(2 * yh, 2)]

        @pl.loop(1, 2 * NR)
        def _(i):
            p = plane_peer(i)
            mine = dsum.at[s, p // 2, pl.ds(2 * lax.rem(p, 2), 2)]
            send(mine, drow.at[s, plane], d_s.at[s, 0], d_r.at[s, 0], at_plane(p))

    def finish(s):
        wait_for(pbuf.at[s], p_r.at[s])
        yfin[...] = ybuf[s, z, :, yh] + pbuf[s]
        for k in range(slots):
            off[s, k] = yfin[pos[s, k]] * (-mask[s, k].astype(F32))

    def diag_z(s):
        wait_for(drow.at[s, pl.ds(0, 2 * NR - 1)], d_r.at[s, 0])
        ebuf[s] = jnp.sum(drow[s], axis=0)
        ez[s, z] = ebuf[s, lax.rem(z, 2)]

        @pl.loop(1, NZ)
        def _(i):
            t = lax.rem(z + i, NZ)
            send(ebuf.at[s, lax.rem(t, 2)], ez.at[s, z], d_s.at[s, 1], d_r.at[s, 1], at_zy(t * 2 + yh))

    tile = r * 4 + yh * 2

    def spread_z(s):
        wait_for(ez.at[s, pl.ds(0, NZ - 1)], d_r.at[s, 1])
        u = tile + lax.rem(z, 2)
        here = gr.at[s, core, u]
        gr[s, core, u] = jnp.sum(ez[s], axis=0)
        send(here, here, d_s.at[s, 2], d_r.at[s, 2], at_zy((z + 1 - 2 * lax.rem(z, 2)) * 2 + yh))

    def spread_row(s):
        wait_for(gr.at[s, core, tile], d_r.at[s, 2])
        here = gr.at[s, core, pl.ds(tile, 2)]

        @pl.loop(1, 2 * NR)
        def _(i):
            send(here, here, d_s.at[s, 3], d_r.at[s, 3], at_plane(plane_peer(i)))

    def spread_core(s):
        wait_for(gr.at[s, core, pl.ds(0, 4 * NR - 2)], d_r.at[s, 3])
        here = gr.at[s, core]
        send(here, here, d_s.at[s, 5], d_r.at[s, 5], mate)

    def gather_diag(s):
        wait_for(gr.at[s, 1 - core], d_r.at[s, 5])
        for h in range(2):
            here = slice(h * lane, (h + 1) * lane)
            diag[s, :, here] = lead[s, :, here] + gr[s, h].reshape(width, lane)

    def leading(s):
        lead[s] = lax.dot_general(
            dinv[s], dinv[s], (((0,), (0,)), ((), ())),
            precision=HIGHEST, preferred_element_type=F32,
        )

    def settle(s):
        wait_for(abuf.at[s, pl.ds(0, NR - 1)], s1_s.at[s])
        wait_for(nbuf.at[pl.ds(0, group), r, pl.ds(0, 2 * NZ - 1), core], s2_s.at[s])
        wait_for(block(s, r), c1_s.at[s])
        for w in range(2):
            wait_for(two(s, 0), c2_s.at[s, w])
            wait_for(block(s, r), c3_s.at[s, w])
        wait_for(nbuf.at[s, :, :, core], sh_s.at[s])
        wait_for(nboth.at[s, 0], n_s.at[s])
        for t in range(NZ - 1):
            wait_for(rbuf.at[s, t], ring_s.at[s, t])
        wait_for(pbuf.at[s], p_s.at[s])

    last = LAG + long_hops
    stages = (
        (2, relay_three), (1, relay_two), (0, relay_one), (3, relay_four), (LAG, multiply),
        (last + 1, diag_row), (last + 2, diag_z), (last + 4, spread_z), (last + 5, spread_row),
        (last + 7, spread_core), (last + 8, gather_diag),
        None,
        (last + 4, finish), (LAG + 1, leading), (last + 4, settle),
    )

    @pl.loop(0, nodes + last + 8)
    def _(n):
        for entry in stages:
            if entry is None:
                @pl.loop(0, long_hops)
                def _(i):
                    t = long_hops - 1 - i
                    s = n - (LAG + 1) - t

                    @pl.when((s >= 0) & (s < nodes))
                    def _():
                        ring(s, t)
            else:
                lag, work = entry
                s = n - lag

                @pl.when((s >= 0) & (s < nodes))
                def _():
                    work(s)

        @pl.when(n == LAG - 1)
        def _():
            wait_for(af.at[core], a_sem.at[0])
            wait_for(af.at[1 - core], a_sem.at[2])

            @pl.loop(0, slots)
            def _(k):
                for h in range(2):
                    rows, cols = ahi.shape[1], ahi.shape[2] // 2
                    high, low = halves(af[h, k].reshape(rows, cols))
                    ahi[k, :, h * cols:(h + 1) * cols] = high
                    alo[k, :, h * cols:(h + 1) * cols] = low

    wait_for(af.at[core], a_sem.at[1])

    @pl.loop(0, nodes)
    def _(s):
        wait_for(drow.at[s, pl.ds(0, 2 * NR - 1)], d_s.at[s, 0])
        wait_for(ez.at[s, pl.ds(0, NZ - 1)], d_s.at[s, 1])
        wait_for(gr.at[s, core, tile], d_s.at[s, 2])
        wait_for(gr.at[s, core, pl.ds(0, 4 * NR - 2)], d_s.at[s, 3])
        wait_for(dmate.at[s], d_s.at[s, 4])
        wait_for(gr.at[s, core], d_s.at[s, 5])


def body(ancestor_inverse, panel, diag_inverse, structure, block_slot):
    nodes, slots, sub, width = panel.shape
    group = 1
    groups = nodes // group
    lane = width // 2
    flat = slots * sub
    blocks = ancestor_inverse.reshape(slots, 2 * NZ, 2, sub, 2 * width)
    rows, depth = width // 2, 4 * width
    smem = pl.BlockSpec(memory_space=pltpu.SMEM)
    hbm = pl.BlockSpec(memory_space=pl.ANY)
    vmem = pl.BlockSpec(memory_space=pltpu.VMEM)
    dma = pltpu.SemaphoreType.DMA
    shapes = (
        jax.ShapeDtypeStruct((nodes, slots, sub, width), F32),
        jax.ShapeDtypeStruct((nodes, width, width), F32),
    )
    off, diag = pl.pallas_call(
        functools.partial(kernel, group),
        out_shape=tuple(pltpu.VMEM(a.shape, F32) for a in shapes),
        in_specs=[smem, smem, hbm, hbm, hbm],
        out_specs=(vmem, vmem),
        scratch_shapes=[
            pltpu.SMEM(block_slot.shape, jnp.int32),
            pltpu.SMEM((nodes, CAP), jnp.int32),
            pltpu.SMEM((nodes, slots), jnp.int32),
            pltpu.SMEM((nodes, slots), jnp.int32),
            pltpu.VMEM((nodes, slots, sub, width), F32),
            pltpu.VMEM((nodes, width, width), F32),
            pltpu.VMEM((2, slots, 2 * NZ, sub, 2 * width), F32),
            pltpu.VMEM((slots, rows, depth), BF16),
            pltpu.VMEM((slots, rows, depth), BF16),
            pltpu.VMEM((nodes, 2, NR, sub, lane), F32),
            pltpu.VMEM((nodes, 2, flat, width), F32),
            pltpu.VMEM((groups, NR, group, 2, sub, lane), F32),
            pltpu.VMEM((nodes, NR, 2 * NZ, 2, sub, lane), F32),
            pltpu.VMEM((depth, width), BF16),
            pltpu.VMEM((depth, width), BF16),
            pltpu.VMEM((nodes, NZ, CAP, 2, sub, width), F32),
            pltpu.VMEM((nodes, NZ - 1, CAP, 2, sub, width), F32),
            pltpu.VMEM((nodes, CAP, sub, width), F32),
            pltpu.VMEM((CAP, sub, width), F32),
            pltpu.VMEM((2 * flat, width), F32),
            pltpu.VMEM((nodes, 2, NR, 4, sub, lane), F32),
            pltpu.VMEM((nodes, NR, 4, sub, lane), F32),
            pltpu.VMEM((nodes, NR, 4, sub, lane), F32),
            pltpu.VMEM((nodes, 2 * NR, 2, sub, lane), F32),
            pltpu.VMEM((nodes, 2, sub, lane), F32),
            pltpu.VMEM((nodes, NZ, sub, lane), F32),
            pltpu.VMEM((nodes, 2, 4 * NR, sub, lane), F32),
            pltpu.VMEM((nodes, width, width), F32),
            dma((2,)), dma((3,)),
            dma((groups,)), dma((groups,)), dma((groups,)),
            dma((groups,)), dma((groups,)), dma((groups,)),
            dma((nodes,)), dma((nodes,)),
            dma((nodes, 2)), dma((nodes, 2)),
            dma((nodes, 2)), dma((nodes, 2)),
            dma((nodes,)), dma((nodes,)),
            dma((nodes,)), dma((nodes,)),
            dma((nodes, NZ - 1)), dma((nodes, NZ - 1)),
            dma((nodes,)), dma((nodes,)),
            dma((nodes, 6)), dma((nodes, 6)),
        ],
        compiler_params=pltpu.CompilerParams(
            collective_id=0, has_side_effects=True, vmem_limit_bytes=61 * 1024 * 1024
        ),
        name="invert_level",
    )(structure, block_slot, blocks, panel, diag_inverse)
    return off, diag


def solution(mesh):
    in_specs = (P("row", "col"), P(None, "row", "col", None), P(), P(), P())
    out_specs = (P(None, "row", "col", None), P())
    return jax.shard_map(body, mesh=mesh, in_specs=in_specs, out_specs=out_specs, check_vma=False)
```

```python
import functools

import jax
import jax.numpy as jnp
from jax import lax
from jax.experimental import pallas as pl
from jax.experimental.pallas import tpu as pltpu
from jax.sharding import PartitionSpec as P

F32 = jnp.float32
BF16 = jnp.bfloat16
MESH = pl.DeviceIdType.MESH
HIGHEST = lax.Precision.HIGHEST

NR = 8
NZ = 8
CAP = 6
LAG = 3


def halves(value):
    high = value.astype(BF16)
    return high, (value - high.astype(F32)).astype(BF16)


def wait_for(ref, sem):
    pltpu.make_async_copy(ref, ref, sem).wait()


def kernel(
    group,
    structure, place, a_ref, panel_ref, dinv_ref, off, diag,
    bits, ids, pos, mask, panel, dinv,
    af, ahi, alo, nsrc, nboth, abuf, nbuf, nhi, nlo, ybuf, rbuf, pbuf, yfin, fexp,
    dbuf, dmate, dsum, drow, ebuf, ez, gr, lead,
    in_sem, a_sem, s1_s, s1_r, s1_l, s2_s, s2_r, s2_l,
    c1_s, c1_r, c2_s, c2_r, c3_s, c3_r, sh_s, sh_r, n_s, n_r,
    ring_s, ring_r, p_s, p_r, d_s, d_r,
):
    nodes, slots, sub, width = panel.shape
    lane = width // 2
    flat = slots * sub
    groups = nodes // group
    r = lax.axis_index("row")
    c = lax.axis_index("col")
    z = c // 4
    yh = lax.rem(c // 2, 2)
    core = lax.rem(c, 2)
    zy = c // 2
    x = r // 2
    yl = lax.rem(r, 2)

    def send(src, dst, ssem, rsem, where):
        pltpu.make_async_remote_copy(
            src_ref=src, dst_ref=dst, send_sem=ssem, recv_sem=rsem,
            device_id=where, device_id_type=MESH,
        ).start()

    def at_row(t):
        return {"row": t, "col": c}

    def at_zy(t):
        return {"row": r, "col": t * 2 + core}

    plane = r * 2 + yh

    def at_plane(t):
        return {"row": t // 2, "col": (z * 2 + lax.rem(t, 2)) * 2 + core}

    plane_peers = [
        lax.rem(r // 2 + dx, 4) * 4 + (lax.rem(r, 2) if dl == 0 else 1 - lax.rem(r, 2)) * 2 + (yh if dh == 0 else 1 - yh)
        for dx, dl, dh in sorted(
            ((dx, dl, dh) for dx in range(4) for dl in range(2) for dh in range(2) if dx or dl or dh),
            key=lambda d: -min(d[0], 4 - d[0]) - (1 if d[1] else 2 * d[2]),
        )
    ]
    z_steps = (4, 3, 5, 2, 6, 1, 7)

    def row_peer(i):
        return lax.rem(r + i, NR)

    def zy_peer(i):
        return lax.rem(zy + i, 2 * NZ)

    mate = {"row": r, "col": zy * 2 + 1 - core}
    across = at_zy(z * 2 + 1 - yh)

    load_panel = pltpu.make_async_copy(panel_ref, panel, in_sem.at[0])
    load_dinv = pltpu.make_async_copy(dinv_ref, dinv, in_sem.at[1])
    own_a = pltpu.make_async_copy(a_ref.at[:, :, core], af.at[core], a_sem.at[0])
    load_panel.start()
    load_dinv.start()
    own_a.start()

    barrier = pltpu.get_barrier_semaphore()

    def greet(where):
        pl.semaphore_signal(barrier, inc=1, device_id=where, device_id_type=MESH)

    @pl.loop(1, 2 * NZ)
    def _(i):
        greet(at_zy(zy_peer(i)))

    @pl.loop(1, NR)
    def _(i):
        greet(at_row(row_peer(i)))
        greet(at_plane(row_peer(i) * 2 + 1 - yh))

    greet(mate)

    for i in range(bits.shape[0]):
        bits[i] = jnp.int32(0)
    for i in range(slots):
        bits[r * slots + i] = jnp.int32(1 << i)

    def mark(s):
        used = bits[place[structure[s, 0]]]
        for k in range(1, structure.shape[1]):
            used = used + bits[place[structure[s, k]]]
        for i in range(slots):
            mask[s, i] = lax.shift_right_logical(used, jnp.int32(i)) & 1

    def normalize(s):
        value = jnp.dot(
            panel[s].reshape(flat, width), dinv[s],
            precision=HIGHEST, preferred_element_type=F32,
        )
        for k in range(slots):
            part = value[k * sub:(k + 1) * sub] * mask[s, k].astype(F32)
            nboth[s, 0, k * sub:(k + 1) * sub, :] = part
            for h in range(2):
                nsrc[s, k // 4, (k % 4) * 2 + h] = part[:, h * lane:(h + 1) * lane]

    mark(0)
    load_panel.wait()
    load_dinv.wait()
    normalize(0)
    pl.semaphore_wait(barrier, 2 * NZ - 1 + 2 * NR - 1)

    def exchange_row(g):
        span = pl.ds(g * group, group)
        pltpu.make_async_copy(nsrc.at[span, :, r], abuf.at[g, r], s1_l.at[g]).start()

        @pl.loop(1, NR)
        def _(i):
            p = lax.rem(r + i, NR)
            send(nsrc.at[span, :, p], abuf.at[g, r], s1_s.at[g], s1_r.at[g], {"row": p, "col": c})

    def exchange_col(g):
        span = pl.ds(g * group, group)
        wait_for(abuf.at[g, r], s1_l.at[g])
        wait_for(abuf.at[g, pl.ds(0, NR - 1)], s1_r.at[g])
        pltpu.make_async_copy(abuf.at[g, z, :, yh], nbuf.at[span, r, zy, core], s2_l.at[g]).start()

        @pl.loop(1, 2 * NZ)
        def _(i):
            t = zy_peer(i)
            send(
                abuf.at[g, t // 2, :, lax.rem(t, 2)], nbuf.at[span, r, zy, core],
                s2_s.at[g], s2_r.at[g], at_zy(t),
            )

    exchange_row(0)
    mark(1)
    normalize(1)
    exchange_row(1)
    send(a_ref.at[:, :, 1 - core], af.at[core], a_sem.at[1], a_sem.at[2], mate)

    @pl.loop(2, nodes)
    def _(s):
        mark(s)
        normalize(s)

    exchange_col(0)

    @pl.loop(0, nodes)
    def _(s):
        before = jnp.int32(0)
        spots = []
        for i in range(slots):
            pos[s, i] = before * mask[s, i]
            spots.append(before)
            before = before + mask[s, i]
        for k in range(CAP):
            found = jnp.int32(0)
            for i in range(slots):
                found = found + i * mask[s, i] * (spots[i] == k).astype(jnp.int32)
            ids[s, k] = found

    @pl.loop(2, groups)
    def _(g):
        exchange_row(g)

    exchange_col(1)

    right = {"row": lax.rem(x + 1, 4) * 2 + yl, "col": c}
    left = {"row": lax.rem(x + 3, 4) * 2 + yl, "col": c}
    other = x * 2 + 1 - yl
    twin = {"row": other, "col": c}
    xl, xr, xo = lax.rem(x + 3, 4), lax.rem(x + 1, 4), lax.rem(x + 2, 4)
    way = 1 - 2 * core
    long_hops, short_hops = NZ // 2, NZ // 2 - 1

    def z_at(d):
        return lax.rem(z + d + NZ, NZ)

    after_long = at_zy(z_at(-way) * 2 + yh)
    after_short = at_zy(z_at(way) * 2 + yh)

    def pass_long(s, t):
        part = ybuf.at[s, z_at(-way * (long_hops - t))]
        send(part, rbuf.at[s, t], ring_s.at[s, t], ring_r.at[s, t], after_long)

    def pass_short(s, t):
        part = ybuf.at[s, z_at(way * (short_hops - t))]
        k = long_hops + t
        send(part, rbuf.at[s, k], ring_s.at[s, k], ring_r.at[s, k], after_short)

    def block(s, p):
        return nbuf.at[s, p, :, core]

    def two(s, p):
        return nbuf.at[s, pl.ds(p, 2), :, core]

    def share(s, part):
        send(part, part, sh_s.at[s], sh_r.at[s], mate)

    def relay_one(s):
        wait_for(nbuf.at[pl.ds(0, group), r, zy, core], s2_l.at[s])
        wait_for(nbuf.at[pl.ds(0, group), r, pl.ds(0, 2 * NZ - 1), core], s2_r.at[s])

        @pl.when(s + 2 < groups)
        def _():
            exchange_col(s + 2)

        mine = block(s, r)
        send(mine, mine, c1_s.at[s], c1_r.at[s], twin)
        send(mine, mine, c2_s.at[s, 0], c2_r.at[s, 0], right)
        send(mine, mine, c2_s.at[s, 1], c2_r.at[s, 1], left)
        share(s, mine)

    def relay_two(s):
        wait_for(block(s, r), c1_r.at[s])
        theirs = block(s, other)
        send(theirs, theirs, c2_s.at[s, 0], c2_r.at[s, 0], right)
        send(theirs, theirs, c2_s.at[s, 1], c2_r.at[s, 1], left)
        share(s, theirs)

    def relay_three(s):
        wait_for(two(s, 0), c2_r.at[s, 0])
        send(block(s, 2 * xl), block(s, 2 * xl), c3_s.at[s, 0], c3_r.at[s, 0], right)
        share(s, two(s, 2 * xl))
        wait_for(two(s, 0), c2_r.at[s, 1])
        send(block(s, 2 * xr + 1), block(s, 2 * xr + 1), c3_s.at[s, 1], c3_r.at[s, 1], left)
        share(s, two(s, 2 * xr))

    def relay_four(s):
        wait_for(block(s, r), c3_r.at[s, 0])
        wait_for(block(s, r), c3_r.at[s, 1])
        share(s, two(s, 2 * xo))

    def multiply(s):
        wait_for(nbuf.at[s, :, :, 1 - core], sh_r.at[s])
        for j in range(4):
            for h in range(2):
                high, low = halves(nbuf[s, 2 * j + h].reshape(width, lane))
                nhi[j * width:(j + 1) * width, h * lane:(h + 1) * lane] = high
                nlo[j * width:(j + 1) * width, h * lane:(h + 1) * lane] = low

        @pl.loop(0, CAP // 2)
        def _(m):
            one, two = ids[s, 2 * m], ids[s, 2 * m + 1]
            high = jnp.concatenate([ahi[one], ahi[two]], axis=0)
            low = jnp.concatenate([alo[one], alo[two]], axis=0)
            total = jnp.dot(high, nhi[...], preferred_element_type=F32)
            total += jnp.dot(high, nlo[...], preferred_element_type=F32)
            total += jnp.dot(low, nhi[...], preferred_element_type=F32)
            rows = ahi.shape[1]
            ybuf[s, :, 2 * m] = total[:rows].reshape(NZ, 2, sub, width)
            ybuf[s, :, 2 * m + 1] = total[rows:].reshape(NZ, 2, sub, width)
        pass_long(s, 0)
        pass_short(s, 0)
        send(nboth.at[s, 0], nboth.at[s, 1], n_s.at[s], n_r.at[s], across)

    def ring(s, t):
        wait_for(rbuf.at[s, t], ring_r.at[s, t])
        b = z_at(-way * (long_hops - 1 - t))
        ybuf[s, b] = ybuf[s, b] + rbuf[s, t]

        @pl.when(t < long_hops - 1)
        def _():
            pass_long(s, t + 1)
            k = long_hops + t
            wait_for(rbuf.at[s, k], ring_r.at[s, k])
            f = z_at(way * (short_hops - 1 - t))
            ybuf[s, f] = ybuf[s, f] + rbuf[s, k]

            @pl.when(t < short_hops - 1)
            def _():
                pass_short(s, t + 1)

        @pl.when(t == long_hops - 1)
        def _():
            send(ybuf.at[s, z, :, 1 - yh], pbuf.at[s], p_s.at[s], p_r.at[s], across)
            wait_for(nboth.at[s, 1], n_r.at[s])
            for k in range(slots):
                scale = mask[s, k].astype(F32)
                fexp[k * sub:(k + 1) * sub, :] = ybuf[s, z, pos[s, k], yh] * scale
                fexp[flat + k * sub:flat + (k + 1) * sub, :] = ybuf[s, z, pos[s, k], 1 - yh] * scale
            part = lax.dot_general(
                nboth[s].reshape(2 * flat, width), fexp[...], (((0,), (0,)), ((), ())),
                precision=HIGHEST, preferred_element_type=F32,
            )
            for h in range(2):
                dbuf[s, h] = part[:, h * lane:(h + 1) * lane].reshape(NR, 4, sub, lane)
            send(dbuf.at[s, 1 - core], dmate.at[s], d_s.at[s, 4], d_r.at[s, 4], mate)

    def diag_row(s):
        wait_for(dmate.at[s], d_r.at[s, 4])
        dsum[s] = dbuf[s, core] + dmate[s]
        drow[s, plane] = dsum[s, r, pl.ds(2 * yh, 2)]

        for p in plane_peers:
            mine = dsum.at[s, p // 2, pl.ds(2 * lax.rem(p, 2), 2)]
            send(mine, drow.at[s, plane], d_s.at[s, 0], d_r.at[s, 0], at_plane(p))

    def finish(s):
        wait_for(pbuf.at[s], p_r.at[s])
        yfin[...] = ybuf[s, z, :, yh] + pbuf[s]
        for k in range(slots):
            off[s, k] = yfin[pos[s, k]] * (-mask[s, k].astype(F32))

    def diag_z(s):
        wait_for(drow.at[s, pl.ds(0, 2 * NR - 1)], d_r.at[s, 0])
        ebuf[s] = jnp.sum(drow[s], axis=0)
        ez[s, z] = ebuf[s, lax.rem(z, 2)]

        for i in z_steps:
            t = lax.rem(z + i, NZ)
            send(ebuf.at[s, lax.rem(t, 2)], ez.at[s, z], d_s.at[s, 1], d_r.at[s, 1], at_zy(t * 2 + yh))

    tile = r * 4 + yh * 2

    def spread_z(s):
        wait_for(ez.at[s, pl.ds(0, NZ - 1)], d_r.at[s, 1])
        u = tile + lax.rem(z, 2)
        here = gr.at[s, core, u]
        gr[s, core, u] = jnp.sum(ez[s], axis=0)
        send(here, here, d_s.at[s, 2], d_r.at[s, 2], at_zy((z + 1 - 2 * lax.rem(z, 2)) * 2 + yh))

    def spread_row(s):
        wait_for(gr.at[s, core, tile], d_r.at[s, 2])
        here = gr.at[s, core, pl.ds(tile, 2)]

        for p in plane_peers:
            send(here, here, d_s.at[s, 3], d_r.at[s, 3], at_plane(p))

    def spread_core(s):
        wait_for(gr.at[s, core, pl.ds(0, 4 * NR - 2)], d_r.at[s, 3])
        here = gr.at[s, core]
        send(here, here, d_s.at[s, 5], d_r.at[s, 5], mate)
        wait_for(drow.at[s, pl.ds(0, 2 * NR - 1)], d_s.at[s, 0])
        wait_for(ez.at[s, pl.ds(0, NZ - 1)], d_s.at[s, 1])
        wait_for(gr.at[s, core, tile], d_s.at[s, 2])
        wait_for(dmate.at[s], d_s.at[s, 4])
        wait_for(gr.at[s, core, pl.ds(0, 4 * NR - 2)], d_s.at[s, 3])

    def gather_diag(s):
        wait_for(gr.at[s, 1 - core], d_r.at[s, 5])
        for h in range(2):
            here = slice(h * lane, (h + 1) * lane)
            diag[s, :, here] = lead[s, :, here] + gr[s, h].reshape(width, lane)

    def leading(s):
        lead[s] = lax.dot_general(
            dinv[s], dinv[s], (((0,), (0,)), ((), ())),
            precision=HIGHEST, preferred_element_type=F32,
        )

    def settle(s):
        wait_for(abuf.at[s, pl.ds(0, NR - 1)], s1_s.at[s])
        wait_for(nbuf.at[pl.ds(0, group), r, pl.ds(0, 2 * NZ - 1), core], s2_s.at[s])
        wait_for(block(s, r), c1_s.at[s])
        for w in range(2):
            wait_for(two(s, 0), c2_s.at[s, w])
            wait_for(block(s, r), c3_s.at[s, w])
        wait_for(nbuf.at[s, :, :, core], sh_s.at[s])
        wait_for(nboth.at[s, 0], n_s.at[s])
        for t in range(NZ - 1):
            wait_for(rbuf.at[s, t], ring_s.at[s, t])
        wait_for(pbuf.at[s], p_s.at[s])

    last = LAG + long_hops
    stages = (
        (2, relay_three), (1, relay_two), (0, relay_one), (3, relay_four), (LAG + 1, leading), (LAG, multiply),
        (last + 1, diag_row), (last + 2, diag_z), (last + 4, spread_z), (last + 5, spread_row),
        (last + 7, spread_core), (last + 8, gather_diag),
        None,
        (last + 4, finish), (last + 4, settle),
    )

    @pl.loop(0, nodes + last + 8)
    def _(n):
        for entry in stages:
            if entry is None:
                @pl.loop(0, long_hops)
                def _(i):
                    t = long_hops - 1 - i
                    s = n - (LAG + 1) - t

                    @pl.when((s >= 0) & (s < nodes))
                    def _():
                        ring(s, t)
            else:
                lag, work = entry
                s = n - lag

                @pl.when((s >= 0) & (s < nodes))
                def _():
                    work(s)

        @pl.when(n == LAG - 1)
        def _():
            wait_for(af.at[core], a_sem.at[0])
            wait_for(af.at[1 - core], a_sem.at[2])

            @pl.loop(0, slots)
            def _(k):
                for h in range(2):
                    rows, cols = ahi.shape[1], ahi.shape[2] // 2
                    high, low = halves(af[h, k].reshape(rows, cols))
                    ahi[k, :, h * cols:(h + 1) * cols] = high
                    alo[k, :, h * cols:(h + 1) * cols] = low

    wait_for(af.at[core], a_sem.at[1])

    @pl.loop(0, nodes)
    def _(s):
        wait_for(gr.at[s, core], d_s.at[s, 5])


def body(ancestor_inverse, panel, diag_inverse, structure, block_slot):
    nodes, slots, sub, width = panel.shape
    group = 1
    groups = nodes // group
    lane = width // 2
    flat = slots * sub
    blocks = ancestor_inverse.reshape(slots, 2 * NZ, 2, sub, 2 * width)
    rows, depth = width // 2, 4 * width
    smem = pl.BlockSpec(memory_space=pltpu.SMEM)
    hbm = pl.BlockSpec(memory_space=pl.ANY)
    vmem = pl.BlockSpec(memory_space=pltpu.VMEM)
    dma = pltpu.SemaphoreType.DMA
    shapes = (
        jax.ShapeDtypeStruct((nodes, slots, sub, width), F32),
        jax.ShapeDtypeStruct((nodes, width, width), F32),
    )
    off, diag = pl.pallas_call(
        functools.partial(kernel, group),
        out_shape=tuple(pltpu.VMEM(a.shape, F32) for a in shapes),
        in_specs=[smem, smem, hbm, hbm, hbm],
        out_specs=(vmem, vmem),
        scratch_shapes=[
            pltpu.SMEM(block_slot.shape, jnp.int32),
            pltpu.SMEM((nodes, CAP), jnp.int32),
            pltpu.SMEM((nodes, slots), jnp.int32),
            pltpu.SMEM((nodes, slots), jnp.int32),
            pltpu.VMEM((nodes, slots, sub, width), F32),
            pltpu.VMEM((nodes, width, width), F32),
            pltpu.VMEM((2, slots, 2 * NZ, sub, 2 * width), F32),
            pltpu.VMEM((slots, rows, depth), BF16),
            pltpu.VMEM((slots, rows, depth), BF16),
            pltpu.VMEM((nodes, 2, NR, sub, lane), F32),
            pltpu.VMEM((nodes, 2, flat, width), F32),
            pltpu.VMEM((groups, NR, group, 2, sub, lane), F32),
            pltpu.VMEM((nodes, NR, 2 * NZ, 2, sub, lane), F32),
            pltpu.VMEM((depth, width), BF16),
            pltpu.VMEM((depth, width), BF16),
            pltpu.VMEM((nodes, NZ, CAP, 2, sub, width), F32),
            pltpu.VMEM((nodes, NZ - 1, CAP, 2, sub, width), F32),
            pltpu.VMEM((nodes, CAP, sub, width), F32),
            pltpu.VMEM((CAP, sub, width), F32),
            pltpu.VMEM((2 * flat, width), F32),
            pltpu.VMEM((nodes, 2, NR, 4, sub, lane), F32),
            pltpu.VMEM((nodes, NR, 4, sub, lane), F32),
            pltpu.VMEM((nodes, NR, 4, sub, lane), F32),
            pltpu.VMEM((nodes, 2 * NR, 2, sub, lane), F32),
            pltpu.VMEM((nodes, 2, sub, lane), F32),
            pltpu.VMEM((nodes, NZ, sub, lane), F32),
            pltpu.VMEM((nodes, 2, 4 * NR, sub, lane), F32),
            pltpu.VMEM((nodes, width, width), F32),
            dma((2,)), dma((3,)),
            dma((groups,)), dma((groups,)), dma((groups,)),
            dma((groups,)), dma((groups,)), dma((groups,)),
            dma((nodes,)), dma((nodes,)),
            dma((nodes, 2)), dma((nodes, 2)),
            dma((nodes, 2)), dma((nodes, 2)),
            dma((nodes,)), dma((nodes,)),
            dma((nodes,)), dma((nodes,)),
            dma((nodes, NZ - 1)), dma((nodes, NZ - 1)),
            dma((nodes,)), dma((nodes,)),
            dma((nodes, 6)), dma((nodes, 6)),
        ],
        compiler_params=pltpu.CompilerParams(
            collective_id=0, has_side_effects=True, vmem_limit_bytes=61 * 1024 * 1024
        ),
        name="invert_level",
    )(structure, block_slot, blocks, panel, diag_inverse)
    return off, diag


def solution(mesh):
    in_specs = (P("row", "col"), P(None, "row", "col", None), P(), P(), P())
    out_specs = (P(None, "row", "col", None), P())
    return jax.shard_map(body, mesh=mesh, in_specs=in_specs, out_specs=out_specs, check_vma=False)
```
